512 devices in a mesh: ctx: 64 (over z, x_lo, core), ch: 8 (over x_hi, y).
Axes of the slice: x: 4 (x_hi: 2, x_lo: 2; x = x_hi * 2 + x_lo), y: 4, z: 16, core: 2. Of those that a mesh axis runs over, the one named last changes fastest.
Arguments:
- q_in: bfloat16 [8192, 8192], P('ctx', 'ch'), may hold values from -6 to 6
- k_in: bfloat16 [8192, 8192], P('ctx', 'ch'), may hold values from -6 to 6
- v_in: bfloat16 [8192, 8192], P('ctx', 'ch'), may hold values from -6 to 6
- stretch_of_slot: int32 [128], replicated, may hold values from 0 to 127, each once
- short_weight: float32 [3, 7, 8192], P(None, None, 'ch'), may hold values from -2 to 2
- rates: float32 [16, 8192], P(None, 'ch'), may hold values from 1.2207031e-06 to 0.03
- residues: float32 [16, 8192], P(None, 'ch'), may hold values from -12 to 12
- skip: float32 [8192], P('ch'), may hold values from -4 to 4
- gain: float32 [8192], P('ch'), may hold values from 0.5 to 1.5
Outputs:
- operator_out: bfloat16 [8192, 8192], P('ctx', 'ch')
The draws below stay inside these ranges and needn't reach their ends.
Inputs may be any that keep to these rules, and one draw needn't show every extreme that they name: stretch_of_slot names every sequence stretch exactly once.
All inputs are finite; a program needn't handle non-finite values.
Results may differ from the reference program's by a relative error of at most 0.001.
Values may be sent and summed in bfloat16 or wider, within the bound.
A program may use at most 64 MiB of HBM per device.

```python
import math
import jax
import jax.numpy as jnp
from jax import lax

D = 8192
ORDER = 16
SHORT = 7
STRETCH = 64
NCHUNK = 128
SEQ = 8192


def draw_residues(key, part):
    ramp = jnp.exp(jnp.log(3.0) * jnp.arange(D, dtype=jnp.float32) / D)
    base = jnp.clip(jax.random.normal(key, (ORDER, D), jnp.float32), -4.0, 4.0)
    return base * ramp[None, :]


def level_of(own_key, shape, cuts, smallest, largest):
    level, own = 1.0, jax.random.fold_in(own_key, 6)
    for axis_at, shards_of in cuts:
        heights = jnp.exp(jax.random.uniform(jax.random.fold_in(own, axis_at), (shards_of,), jnp.float32, smallest / len(cuts), largest / len(cuts)))
        level = level * jnp.repeat(heights, shape[axis_at] // shards_of).reshape([-1 if axis == axis_at else 1 for axis in range(len(shape))])
    return level


def scatter_about(stream_key, dims, scale, limit, shards=(), held_as=jnp.bfloat16):
    factor_of = level_of(stream_key, dims, shards, -0.22, 0.18) if shards else 1.0
    drawn = jax.random.normal(stream_key, dims, jnp.float32) * scale * factor_of
    return jnp.minimum(jnp.maximum(drawn, -limit), limit).astype(held_as)


def setup_inputs(seed: int = 0) -> dict:
    streams_of = jax.random.split(jax.random.key(seed), 10)
    return {
        "q_in": scatter_about(streams_of[0], (SEQ, D), 1.0, 6.0, ((0, 64), (1, 8))),
        "k_in": scatter_about(streams_of[1], (SEQ, D), 1.0, 6.0, ((0, 64), (1, 8))),
        "v_in": scatter_about(streams_of[2], (SEQ, D), 1.0, 6.0, ((0, 64), (1, 8))),
        "stretch_of_slot": jax.random.permutation(streams_of[3], NCHUNK).astype(jnp.int32),
        "short_weight": scatter_about(streams_of[4], (3, SHORT, D), SHORT ** -0.5, 2.0, ((2, 8),), jnp.float32),
        "rates": jnp.clip(jnp.exp(math.log(0.03) - 10.109526 * jax.random.uniform(streams_of[5], (ORDER, D), jnp.float32) ** level_of(streams_of[5], (ORDER, D), ((1, 8),), -0.2, 0.2)), 1.220703097715159e-06, 0.03),
        "residues": draw_residues(jax.random.fold_in(streams_of[9], 71), 0),
        "skip": scatter_about(streams_of[7], (D,), 1.0, 4.0, ((0, 8),), jnp.float32),
        "gain": jnp.clip(1.0 + 0.1 * jax.random.normal(streams_of[8], (D,), jnp.float32), 0.5, 1.5),
    }


def reference(q_in, k_in, v_in, stretch_of_slot, short_weight, rates, residues, skip, gain):
    inverse = jnp.zeros((NCHUNK,), jnp.int32).at[stretch_of_slot].set(jnp.arange(NCHUNK, dtype=jnp.int32))

    def ordered(values):
        return values.reshape(NCHUNK, STRETCH, D)[inverse].reshape(SEQ, D)
    q_seq = ordered(q_in)
    k_seq = ordered(k_in)
    v_seq = ordered(v_in)
    width = min(D, 512)
    groups = D // width

    def columns(values, group):
        return lax.dynamic_slice_in_dim(values, group * width, width, values.ndim - 1)

    def short_conv(values, taps):
        padded = jnp.pad(values.astype(jnp.float32), ((SHORT - 1, 0), (0, 0)))
        total = jnp.zeros((SEQ, width), jnp.float32)
        for shift_by in range(SHORT):
            total = total + taps[shift_by][None, :] * padded[SHORT - 1 - shift_by:SHORT - 1 - shift_by + SEQ]
        return total

    def one_group(group):
        taps = columns(short_weight, group)
        query = short_conv(columns(q_seq, group), taps[0])
        keys = short_conv(columns(k_seq, group), taps[1])
        values = short_conv(columns(v_seq, group), taps[2])
        mixed_in = keys * values
        rate = columns(rates, group)
        scaled = columns(residues, group) * jnp.sqrt(-jnp.expm1(-2.0 * rate))
        times = jnp.arange(SEQ, dtype=jnp.float32)
        filt = jnp.zeros((SEQ, width), jnp.float32)
        for mode in range(ORDER):
            filt = filt + scaled[mode][None, :] * jnp.exp(-rate[mode][None, :] * times[:, None])
        length = 2 * SEQ
        spectrum = jnp.fft.rfft(mixed_in, length, axis=0) * jnp.fft.rfft(filt, length, axis=0)
        conv = jnp.fft.irfft(spectrum, length, axis=0)[:SEQ]
        output = conv + columns(skip, group)[None, :] * mixed_in
        return query * output
    blocks = lax.map(one_group, jnp.arange(groups, dtype=jnp.int32))
    zvalues = blocks.transpose(1, 0, 2).reshape(SEQ, D)
    scale = lax.rsqrt(lax.optimization_barrier(jnp.mean(zvalues * zvalues, axis=1, keepdims=True)) + 1e-05)
    normed = (zvalues * scale * gain[None, :]).astype(jnp.bfloat16)
    return normed.reshape(NCHUNK, STRETCH, D)[stretch_of_slot].reshape(SEQ, D)
```

```python
import jax
import jax.numpy as jnp
from jax import lax
from jax.experimental import pallas as pl
from jax.experimental.pallas import tpu as pltpu
from jax.sharding import PartitionSpec as P

F32 = jnp.float32
BF16 = jnp.bfloat16
MESH = pl.DeviceIdType.MESH
HIGHEST = lax.Precision.HIGHEST

TOKENS = 128
WIDTH = 1024
STRETCH = 64
REACH = 6
TAPS = 7
ORDER = 16
OWNERS = 64
GROUP = 16
SLOTS = 128
EXT = STRETCH + REACH
PAD = 8
EPS = 1e-05


def iota(shape, dim):
    return lax.broadcasted_iota(jnp.int32, shape, dim)


def swap_groups(regs):
    regs = list(regs)
    group = iota((8, 128), 1) // GROUP
    for bit in (1, 2, 4):
        low = (group & bit) == 0
        for i in range(8):
            if i & bit:
                continue
            x, y = regs[i], regs[i | bit]
            regs[i] = jnp.where(low, x, pltpu.roll(y, GROUP * bit, 1))
            regs[i | bit] = jnp.where(low, pltpu.roll(x, 128 - GROUP * bit, 1), y)
    return regs


def one_minus_exp_neg(x):
    series = 1.0 - x / 9.0
    for n in (8, 7, 6, 5, 4, 3, 2):
        series = 1.0 - (x / n) * series
    return jnp.where(x < 0.3, x * series, 1.0 - jnp.exp(-x))


def kernel(
    n_ch,
    width_all,
    q_ref,
    k_ref,
    v_ref,
    sos_ref,
    sw_ref,
    rates_ref,
    res_ref,
    skip_ref,
    gain_ref,
    o_ref,
    ext,
    u_s,
    y_s,
    z_s,
    zn_s,
    rt,
    am,
    sw,
    filt,
    stage,
    own,
    six,
    pb,
    qt,
    pe,
    qs,
    mm,
    scan_s,
    sq_s,
    send_b,
    send_e,
    send_t,
    send_s,
    recv_b,
    recv_e,
    recv_t,
    recv_s,
    sq_send,
    sq_recv,
    ssem,
    rsem,
):
    me = lax.axis_index("ctx")
    my_ch = lax.axis_index("ch")
    my_z, my_l = me // 4, me % 4
    my_sub, my_lg = me // 8, me % 8

    barrier = pltpu.get_barrier_semaphore()

    @pl.loop(1, OWNERS)
    def _(i):
        pl.semaphore_signal(
            barrier, 1, device_id={"ctx": (me + i) % OWNERS}, device_id_type=MESH
        )

    @pl.loop(1, n_ch)
    def _(i):
        pl.semaphore_signal(
            barrier, 1, device_id={"ch": (my_ch + i) % n_ch}, device_id_type=MESH
        )

    def send_all(src, dst, sem):
        def one(d):
            pltpu.make_async_remote_copy(
                src_ref=src.at[d],
                dst_ref=dst.at[me],
                send_sem=ssem.at[sem],
                recv_sem=rsem.at[sem],
                device_id={"ctx": d},
                device_id_type=MESH,
            ).start()

        @pl.loop(0, 15)
        def _(i):
            step = 15 - i
            far = (step + 1) // 2
            d_z = (my_z + (2 * (step % 2) - 1) * far + 16) % 16
            for l in range(4):
                one(d_z * 4 + (my_l + l) % 4)

        for l in range(1, 4):
            one(my_z * 4 + (my_l + l) % 4)

    def all_of(src, dst, sem):
        return pltpu.make_async_remote_copy(
            src_ref=src.at[pl.ds(0, OWNERS - 1)],
            dst_ref=dst.at[pl.ds(0, OWNERS - 1)],
            send_sem=ssem.at[sem],
            recv_sem=rsem.at[sem],
            device_id={"ctx": (me + 1) % OWNERS},
            device_id_type=MESH,
        )

    def stage_to_send(dst):
        @pl.loop(0, 8)
        def _(b):
            for i in range(8):
                d = b * 8 + i
                dst[d] = stage[pl.ds(pl.multiple_of(d * 8, 8), 8), :].astype(BF16)

    def recv_to_stage(src):
        @pl.loop(0, 8)
        def _(b):
            for i in range(8):
                d = b * 8 + i
                stage[pl.ds(pl.multiple_of(d * 8, 8), 8), :] = src[d].astype(F32)

    def token(array, slot, t):
        return ext[array, pl.ds(pl.multiple_of((slot * EXT + REACH + t) * 8, 8), 8), :]

    def row8(ref, i):
        return ref[pl.ds(pl.multiple_of(i * 8, 8), 8), :]

    for array, ref in ((1, k_ref), (2, v_ref), (0, q_ref)):
        for slot in range(2):

            @pl.loop(0, 4)
            def _(tb):
                for j in range(8):
                    rows = ref[
                        pl.ds(pl.multiple_of(slot * STRETCH + tb * 16, 16), 16),
                        128 * j : 128 * j + 128,
                    ].astype(F32)
                    start = (slot * EXT + REACH + tb * 16) * 8 + j
                    ext[array, pl.ds(start, 16, stride=8), :] = rows

    for j in range(8):
        lanes = slice(128 * j, 128 * j + 128)
        rate = rates_ref[:, lanes]
        amount = res_ref[:, lanes] * jnp.sqrt(one_minus_exp_neg(2.0 * rate))
        rt[pl.ds(j, ORDER, stride=8), :] = rate
        am[pl.ds(j, ORDER, stride=8), :] = amount
        for a in range(3):
            sw[pl.ds(a * 64 + j, TAPS, stride=8), :] = sw_ref[a, :, lanes]
    for a in range(3):
        sw[a * 64 + 56 : a * 64 + 64, :] = jnp.zeros((8, 128), F32)

    for slot in range(2):
        kinds = (
            [token(1, slot, t) for t in range(6)] + [token(0, slot, 58), token(0, slot, 59)],
            [token(2, slot, t) for t in range(6)] + [token(0, slot, 60), token(0, slot, 61)],
            [token(0, slot, 62), token(0, slot, 63)] + [token(1, slot, 58 + t) for t in range(6)],
            [token(0, slot, 62), token(0, slot, 63)] + [token(2, slot, 58 + t) for t in range(6)],
        )
        for kind in range(4):
            for lg, reg in enumerate(swap_groups(kinds[kind])):
                stage[pl.ds(lg * 8 + slot * 4 + kind, 8, stride=64), :] = reg
    stage_to_send(send_b)

    def feature(array, slot, t):
        total = row8(sw, array * 8) * token(array, slot, t)
        for j in range(1, TAPS):
            total = total + row8(sw, array * 8 + j) * token(array, slot, t - j)
        return total

    def u_row(slot, t):
        return pl.ds(pl.multiple_of((slot * STRETCH + t) * 8, 8), 8)

    decay = [jnp.exp(-row8(rt, m)) for m in range(ORDER)]
    for slot in range(2):

        def step(t, acc):
            u = feature(1, slot, t) * feature(2, slot, t)
            u_s[u_row(slot, t), :] = u
            return tuple(a * d + u for a, d in zip(acc, decay))

        ends = lax.fori_loop(
            REACH, STRETCH, step, tuple(jnp.zeros((8, 128), F32) for _ in range(ORDER))
        )
        for h in range(2):
            for lg, reg in enumerate(swap_groups(ends[8 * h : 8 * h + 8])):
                hi = reg.astype(BF16).astype(F32)
                stage[pl.ds(lg * 8 + slot * 4 + 2 * h, 8, stride=64), :] = hi
                stage[pl.ds(lg * 8 + slot * 4 + 2 * h + 1, 8, stride=64), :] = reg - hi
    stage_to_send(send_e)

    pl.semaphore_wait(barrier, OWNERS - 1 + n_ch - 1)
    send_all(send_b, recv_b, 0)
    send_all(send_e, recv_e, 1)
    recv_b[me] = send_b[me]
    recv_e[me] = send_e[me]

    sos = jnp.broadcast_to(sos_ref[...].astype(F32), (SLOTS, SLOTS)).astype(BF16)
    spread = (iota((SLOTS, 512), 0) == iota((SLOTS, 512), 1) // 4).astype(F32).astype(BF16)
    sos_row = jnp.dot(sos[:16], spread, preferred_element_type=F32)[:1].astype(jnp.int32)
    spread_t = (iota((512, SLOTS), 1) == iota((512, SLOTS), 0) // 4).astype(F32).astype(BF16)
    scan_s[...] = lax.dot_general(
        spread_t, sos, (((1,), (1,)), ((), ())), preferred_element_type=F32
    )
    lane = iota((16, 512), 1)
    sublane = iota((16, 512), 0)
    sos_lane = jnp.broadcast_to(sos_row, (16, 512))

    @pl.loop(0, 32)
    def _(b):
        rows = pl.ds(pl.multiple_of(b * 16, 16), 16)
        row = sublane + b * 16
        here = scan_s[rows, :1].astype(jnp.int32)
        kind, s = row // SLOTS, row % SLOTS
        want = s - kind // 2
        hit = ((lane % 4) == kind) & (sos_lane == want)
        pb[rows, :] = hit.astype(F32).astype(BF16)
        hit = ((lane % 4) == row % 4) & (sos_lane == here - 1)
        qt[rows, :] = hit.astype(F32).astype(BF16)
        goal = (row % 2) * 256 + ((row % 4) // 2) * 128 + here - 1
        hit = (lane == goal) & (here > 0)
        qs[rows, :] = hit.astype(F32).astype(BF16)

    @pl.loop(0, 16)
    def _(b):
        rows = pl.ds(pl.multiple_of(b * 16, 16), 16)
        row = sublane + b * 16
        hit = ((lane % 4) // 2 == row // SLOTS) & (sos_lane == row % SLOTS)
        pe[rows, :] = hit.astype(F32).astype(BF16)

    own_rates = []
    for h in range(2):
        for lg, reg in enumerate(swap_groups([row8(rt, 8 * h + m) for m in range(8)])):
            own[lg * 8 : lg * 8 + 8, :] = reg
        own_rates.append(own[pl.ds(my_lg * 8 + my_sub, 1), :])

    lane128 = iota((8, 128), 1)

    def own_taps(array):
        rows = sw[pl.ds(array * 64 + my_sub, 8, stride=8), :]
        rows = pltpu.roll(rows, (128 - GROUP * my_lg) % 128, 1)
        rows = jnp.where(lane128 < GROUP, rows, 0.0)
        for shift in (16, 32, 64):
            rows = rows + pltpu.roll(rows, shift, 1)
        return rows

    taps_k, taps_v = own_taps(1), own_taps(2)
    r_row, r_lane = iota((128, 128), 0), iota((128, 128), 1)
    same = (r_row % GROUP == r_lane % GROUP) & (r_row // GROUP < REACH)
    ago = (STRETCH - 1 - r_row // GROUP).astype(F32)
    for h in range(2):
        mm[:, 128 * h : 128 * h + 128] = jnp.where(same, jnp.exp(-own_rates[h] * ago), 0.0)

    filt[0 : PAD * 8, :] = jnp.zeros((PAD * 8, 128), F32)

    def filter_step(d, powers):
        total = powers[0]
        for p in powers[1:]:
            total = total + p
        filt[pl.ds(pl.multiple_of((d + PAD) * 8, 8), 8), :] = total
        return tuple(p * x for p, x in zip(powers, decay))

    lax.fori_loop(0, STRETCH, filter_step, tuple(row8(am, m) for m in range(ORDER)))

    skip = skip_ref[...]

    @pl.loop(0, 8)
    def _(b):
        t0 = b * 8

        def inner(s, acc):
            taps = [row8(filt, t0 + i - s + PAD) for i in range(8)]
            out = []
            for slot in range(2):
                u = u_s[u_row(slot, s), :]
                out += [acc[slot * 8 + i] + taps[i] * u for i in range(8)]
            return tuple(out)

        acc = lax.fori_loop(
            REACH, t0 + 8, inner, tuple(jnp.zeros((8, 128), F32) for _ in range(16))
        )
        for slot in range(2):
            for i in range(8):
                y_s[u_row(slot, t0 + i), :] = acc[slot * 8 + i]

    for slot in range(2):

        @pl.loop(REACH, STRETCH)
        def _(t):
            z_s[u_row(slot, t), :] = feature(0, slot, t)
            rows = u_row(slot, t)
            y_s[rows, :] = y_s[rows, :] + skip * u_s[rows, :]

    all_of(send_b, recv_b, 0).wait_recv()
    recv_to_stage(recv_b)
    raw = stage[...].astype(BF16)
    stage[...] = jnp.dot(qt[...], raw, preferred_element_type=F32)
    stage_to_send(send_t)
    send_all(send_t, recv_t, 2)
    recv_t[me] = send_t[me]
    stage[...] = jnp.dot(pb[...], raw, preferred_element_type=F32)
    group16 = iota((16, 128), 1) // GROUP

    @pl.loop(0, 8)
    def _(b):
        def edge(kind, taps):
            head = stage[pl.ds(pl.multiple_of(kind * 128 + b * 16, 16), 16), :]
            tail = stage[pl.ds(pl.multiple_of(kind * 128 + 256 + b * 16, 16), 16), :]
            total = taps[0:1] * head
            for j in range(1, TAPS):
                mixed = jnp.where(group16 < 8 - j, head, tail)
                total = total + taps[j : j + 1] * pltpu.roll(mixed, GROUP * j, 1)
            return total

        six[pl.ds(pl.multiple_of(b * 16, 16), 16), :] = edge(0, taps_k) * edge(1, taps_v)

    extra = jnp.dot(six[...], mm[...], precision=HIGHEST, preferred_element_type=F32)

    all_of(send_e, recv_e, 1).wait_recv()
    recv_to_stage(recv_e)
    ends_seq = jnp.dot(pe[...], stage[...].astype(BF16), preferred_element_type=F32)
    sub8 = iota((8, 128), 0)
    for h in range(2):
        x = ends_seq[128 * h : 128 * h + 128] + extra[:, 128 * h : 128 * h + 128]
        span = own_rates[h] * float(STRETCH)
        blocks = [x[8 * b : 8 * b + 8] for b in range(16)]
        for d in (1, 2, 4):
            mult = jnp.where(sub8 >= d, jnp.exp(-span * float(d)), 0.0)
            blocks = [x + mult * pltpu.roll(x, d, 0) for x in blocks]
        lift = jnp.exp(-span * (sub8 + 1).astype(F32))
        whole = jnp.broadcast_to(jnp.exp(-span * 8.0), (8, 128))
        carry = jnp.zeros((8, 128), F32)
        for b in range(16):
            total = jnp.broadcast_to(blocks[b][7:8], (8, 128))
            done = blocks[b] + lift * carry
            carry = whole * carry + total
            hi = done.astype(BF16).astype(F32)
            scan_s[128 * h + 8 * b : 128 * h + 8 * b + 8, :] = hi
            scan_s[256 + 128 * h + 8 * b : 256 + 128 * h + 8 * b + 8, :] = done - hi
    stage[...] = jnp.dot(qs[...], scan_s[...].astype(BF16), preferred_element_type=F32)
    stage_to_send(send_s)
    send_all(send_s, recv_s, 3)
    recv_s[me] = send_s[me]

    all_of(send_t, recv_t, 2).wait_recv()
    recv_to_stage(recv_t)
    for slot in range(2):
        kinds = [
            swap_groups([stage[pl.ds(lg * 8 + slot * 4 + kind, 8, stride=64), :] for lg in range(8)])
            for kind in range(4)
        ]
        tails = (
            kinds[0][6:8] + kinds[1][6:8] + kinds[2][0:2],
            kinds[2][2:8],
            kinds[3][2:8],
        )
        for array in range(3):
            for t in range(6):
                base = (slot * EXT + t) * 8
                ext[array, base : base + 8, :] = tails[array][t]

    for slot in range(2):
        first = []
        for t in range(REACH):
            u = feature(1, slot, t) * feature(2, slot, t)
            first.append(u)
            z_s[u_row(slot, t), :] = feature(0, slot, t)
            rows = u_row(slot, t)
            y_s[rows, :] = y_s[rows, :] + skip * u

        @pl.loop(0, STRETCH)
        def _(t):
            rows = u_row(slot, t)
            total = y_s[rows, :]
            for s in range(REACH):
                total = total + row8(filt, t - s + PAD) * first[s]
            y_s[rows, :] = total

    all_of(send_s, recv_s, 3).wait_recv()
    recv_to_stage(recv_s)
    for slot in range(2):
        starts = []
        for h in range(2):
            base = slot * 4 + 2 * h
            starts += swap_groups(
                [
                    stage[pl.ds(lg * 8 + base, 8, stride=64), :]
                    + stage[pl.ds(lg * 8 + base + 1, 8, stride=64), :]
                    for lg in range(8)
                ]
            )

        def last(t, state):
            state = tuple(x * d for x, d in zip(state, decay))
            even, odd = state[0], state[1]
            for m in range(2, ORDER, 2):
                even, odd = even + state[m], odd + state[m + 1]
            rows = u_row(slot, t)
            z_s[rows, :] = z_s[rows, :] * (y_s[rows, :] + (even + odd))
            return state

        lax.fori_loop(
            0, STRETCH, last, tuple(s * row8(am, m) for m, s in enumerate(starts))
        )

    @pl.loop(0, 16)
    def _(b):
        rows = pl.ds(pl.multiple_of(b * 8, 8), 8)
        total = jnp.zeros((8, 128), F32)
        for j in range(8):
            z = z_s[pl.ds(b * 64 + j, 8, stride=8), :]
            zn_s[rows, 128 * j : 128 * j + 128] = z
            total = total + z * z
        sq_s[rows, :] = total

    sums = lax.dot_general(
        jnp.ones((8, 128), F32),
        sq_s[...],
        (((1,), (1,)), ((), ())),
        precision=HIGHEST,
        preferred_element_type=F32,
    )
    sq_send[0] = sums
    sq_recv[my_ch] = sums

    @pl.loop(1, n_ch)
    def _(i):
        pltpu.make_async_remote_copy(
            src_ref=sq_send.at[0],
            dst_ref=sq_recv.at[my_ch],
            send_sem=ssem.at[4],
            recv_sem=rsem.at[4],
            device_id={"ch": (my_ch + i) % n_ch},
            device_id_type=MESH,
        ).start()

    every = pltpu.make_async_remote_copy(
        src_ref=sq_recv.at[pl.ds(0, n_ch - 1)],
        dst_ref=sq_recv.at[pl.ds(0, n_ch - 1)],
        send_sem=ssem.at[4],
        recv_sem=rsem.at[4],
        device_id={"ch": (my_ch + 1) % n_ch},
        device_id_type=MESH,
    )
    every.wait_recv()
    total = sq_recv[0]
    for i in range(1, n_ch):
        total = total + sq_recv[i]
    scale = lax.rsqrt(total / float(width_all) + EPS)
    sq_s[...] = jnp.transpose(jnp.broadcast_to(scale[0:1], (128, 128)))

    @pl.loop(0, 8)
    def _(b):
        rows = pl.ds(pl.multiple_of(b * 16, 16), 16)
        by = sq_s[rows, :]
        for j in range(8):
            lanes = slice(128 * j, 128 * j + 128)
            o_ref[rows, lanes] = (zn_s[rows, lanes] * by * gain_ref[:, lanes]).astype(BF16)

    all_of(send_b, recv_b, 0).wait_send()
    all_of(send_e, recv_e, 1).wait_send()
    all_of(send_t, recv_t, 2).wait_send()
    all_of(send_s, recv_s, 3).wait_send()
    every.wait_send()


def on_device(n_ch, width_all, q_in, k_in, v_in, stretch_of_slot, short_weight, rates, residues, skip, gain):
    vmem = pl.BlockSpec(memory_space=pltpu.VMEM)
    f32 = lambda *shape: pltpu.VMEM(shape, F32)
    bf16 = lambda *shape: pltpu.VMEM(shape, BF16)
    scratch = (
        [f32(3, 2 * EXT * 8, 128)]
        + [f32(TOKENS * 8, 128)] * 3
        + [f32(TOKENS, WIDTH)]
        + [f32(ORDER * 8, 128)] * 2
        + [f32(192, 128), f32((STRETCH + PAD) * 8, 128), f32(512, 128), f32(64, 128), f32(128, 128)]
        + [bf16(512, 512), bf16(512, 512), bf16(256, 512), bf16(512, 512)]
        + [f32(128, 256), f32(512, 128), f32(128, 128)]
        + [bf16(OWNERS, 8, 128)] * 8
        + [f32(1, 8, 128), f32(n_ch, 8, 128)]
        + [pltpu.SemaphoreType.DMA((5,)), pltpu.SemaphoreType.DMA((5,))]
    )
    import functools

    return pl.pallas_call(
        functools.partial(kernel, n_ch, width_all),
        out_shape=jax.ShapeDtypeStruct((TOKENS, WIDTH), BF16),
        in_specs=[vmem] * 9,
        out_specs=vmem,
        scratch_shapes=scratch,
        compiler_params=pltpu.CompilerParams(collective_id=0, has_side_effects=True),
        name="hyena",
    )(
        q_in,
        k_in,
        v_in,
        stretch_of_slot.reshape(1, SLOTS),
        short_weight,
        rates,
        residues,
        skip.reshape(8, 128),
        gain.reshape(1, WIDTH),
    )


def solution(mesh):
    n_ch = mesh.shape["ch"]

    def body(*args):
        return on_device(n_ch, n_ch * WIDTH, *args)

    in_specs = (
        P("ctx", "ch"),
        P("ctx", "ch"),
        P("ctx", "ch"),
        P(),
        P(None, None, "ch"),
        P(None, "ch"),
        P(None, "ch"),
        P("ch"),
        P("ch"),
    )
    return jax.shard_map(
        body, mesh=mesh, in_specs=in_specs, out_specs=P("ctx", "ch"), check_vma=False
    )
```

```python
import functools

import jax
import jax.numpy as jnp
from jax import lax
from jax.experimental import pallas as pl
from jax.experimental.pallas import tpu as pltpu
from jax.sharding import PartitionSpec as P

F32 = jnp.float32
BF16 = jnp.bfloat16
MESH = pl.DeviceIdType.MESH
HIGHEST = lax.Precision.HIGHEST

TOKENS = 128
WIDTH = 1024
STRETCH = 64
REACH = 6
TAPS = 7
ORDER = 16
OWNERS = 64
GROUP = 16
SLOTS = 128
EXT = STRETCH + REACH
PAD = 8
EPS = 1e-05
FULL = 32000.0
TINY = 1e-30


def iota(shape, dim):
    return lax.broadcasted_iota(jnp.int32, shape, dim)


def swap_groups(regs):
    regs = list(regs)
    group = iota((8, 128), 1) // GROUP
    for bit in (1, 2, 4):
        low = (group & bit) == 0
        for i in range(8):
            if i & bit:
                continue
            x, y = regs[i], regs[i | bit]
            regs[i] = jnp.where(low, x, pltpu.roll(y, GROUP * bit, 1))
            regs[i | bit] = jnp.where(low, pltpu.roll(x, 128 - GROUP * bit, 1), y)
    return regs


def one_minus_exp_neg(x):
    series = 1.0 - x / 9.0
    for n in (8, 7, 6, 5, 4, 3, 2):
        series = 1.0 - (x / n) * series
    return jnp.where(x < 0.3, x * series, 1.0 - jnp.exp(-x))


def kernel(
    n_ch,
    width_all,
    q_hbm,
    k_hbm,
    v_hbm,
    sos_hbm,
    sw_hbm,
    rates_hbm,
    res_hbm,
    skip_hbm,
    gain_hbm,
    o_ref,
    q_ref,
    k_ref,
    v_ref,
    sos_ref,
    sw_ref,
    rates_ref,
    res_ref,
    skip_ref,
    gain_ref,
    ext,
    u_s,
    y_s,
    z_s,
    zn_s,
    rt,
    am,
    sw,
    filt,
    stage,
    own,
    six,
    pb,
    qt,
    pe,
    qs,
    mm,
    scan_s,
    scale_s,
    col_t,
    col_s,
    sq_s,
    send_b,
    send_t,
    recv_b,
    recv_t,
    send_e,
    send_s,
    recv_e,
    recv_s,
    send_x,
    recv_x,
    sq_send,
    sq_recv,
    ssem,
    rsem,
    isem,
):
    me = lax.axis_index("ctx")
    my_ch = lax.axis_index("ch")
    my_z, my_l = me // 4, me % 4
    my_sub, my_lg = me // 8, me % 8

    barrier = pltpu.get_barrier_semaphore()

    @pl.loop(1, OWNERS)
    def _(i):
        pl.semaphore_signal(
            barrier, 1, device_id={"ctx": (me + i) % OWNERS}, device_id_type=MESH
        )

    @pl.loop(1, n_ch)
    def _(i):
        pl.semaphore_signal(
            barrier, 1, device_id={"ch": (my_ch + i) % n_ch}, device_id_type=MESH
        )

    def load(i, src, dst):
        copy = pltpu.make_async_copy(src, dst, isem.at[i])
        copy.start()
        return copy

    loads = {
        "rates": load(0, rates_hbm, rates_ref),
        "res": load(1, res_hbm, res_ref),
        "sw": load(2, sw_hbm, sw_ref),
        "k": load(3, k_hbm, k_ref),
        "v": load(4, v_hbm, v_ref),
        "q": load(5, q_hbm, q_ref),
        "sos": load(6, sos_hbm, sos_ref),
        "skip": load(7, skip_hbm, skip_ref),
        "gain": load(8, gain_hbm, gain_ref),
    }

    def send_all(src, dst, sem):
        def one(d):
            pltpu.make_async_remote_copy(
                src_ref=src.at[d],
                dst_ref=dst.at[me],
                send_sem=ssem.at[sem],
                recv_sem=rsem.at[sem],
                device_id={"ctx": d},
                device_id_type=MESH,
            ).start()

        @pl.loop(0, 15)
        def _(i):
            step = 15 - i
            far = (step + 1) // 2
            d_z = (my_z + (2 * (step % 2) - 1) * far + 16) % 16
            for l in range(4):
                one(d_z * 4 + (my_l + l) % 4)

        for l in range(1, 4):
            one(my_z * 4 + (my_l + l) % 4)

    def all_of(src, dst, sem):
        return pltpu.make_async_remote_copy(
            src_ref=src.at[pl.ds(0, OWNERS - 1)],
            dst_ref=dst.at[pl.ds(0, OWNERS - 1)],
            send_sem=ssem.at[sem],
            recv_sem=rsem.at[sem],
            device_id={"ctx": (me + 1) % OWNERS},
            device_id_type=MESH,
        )

    def code(x):
        return x.astype(jnp.int32).astype(jnp.int16)

    def uncode(x):
        return x.astype(jnp.int32).astype(F32)

    def narrow(x):
        return x.astype(BF16)

    def widen(x):
        return x.astype(F32)

    def stage_to_send(dst, pitch, first, convert):
        rows = dst.shape[1]

        @pl.loop(0, 8)
        def _(b):
            for i in range(8):
                d = b * 8 + i
                dst[d] = convert(stage[pl.ds(d * pitch + first, rows), :])

    def recv_to_stage(src, pitch, first, convert):
        rows = src.shape[1]

        @pl.loop(0, 8)
        def _(b):
            for i in range(8):
                d = b * 8 + i
                stage[pl.ds(d * pitch + first, rows), :] = convert(src[d])

    def token(array, slot, t):
        return ext[array, pl.ds(pl.multiple_of((slot * EXT + REACH + t) * 8, 8), 8), :]

    def row8(ref, i):
        return ref[pl.ds(pl.multiple_of(i * 8, 8), 8), :]

    loads["rates"].wait()
    loads["res"].wait()
    loads["sw"].wait()
    for j in range(8):
        lanes = slice(128 * j, 128 * j + 128)
        rate = rates_ref[:, lanes]
        amount = res_ref[:, lanes] * jnp.sqrt(one_minus_exp_neg(2.0 * rate))
        rt[pl.ds(j, ORDER, stride=8), :] = rate
        am[pl.ds(j, ORDER, stride=8), :] = amount
        for a in range(3):
            sw[pl.ds(a * 64 + j, TAPS, stride=8), :] = sw_ref[a, :, lanes]
    for a in range(3):
        sw[a * 64 + 56 : a * 64 + 64, :] = jnp.zeros((8, 128), F32)

    for array, name, ref in ((1, "k", k_ref), (2, "v", v_ref), (0, "q", q_ref)):
        loads[name].wait()
        for slot in range(2):

            @pl.loop(0, 4)
            def _(tb):
                for j in range(8):
                    rows = ref[
                        pl.ds(pl.multiple_of(slot * STRETCH + tb * 16, 16), 16),
                        128 * j : 128 * j + 128,
                    ].astype(F32)
                    start = (slot * EXT + REACH + tb * 16) * 8 + j
                    ext[array, pl.ds(start, 16, stride=8), :] = rows
    loads["sos"].wait()
    loads["skip"].wait()
    loads["gain"].wait()

    def feature(array, slot, t):
        total = row8(sw, array * 8) * token(array, slot, t)
        for j in range(1, TAPS):
            total = total + row8(sw, array * 8 + j) * token(array, slot, t - j)
        return total

    def u_row(slot, t):
        return pl.ds(pl.multiple_of((slot * STRETCH + t) * 8, 8), 8)

    decay = [jnp.exp(-row8(rt, m)) for m in range(ORDER)]
    end_scale = []
    for slot in range(2):

        def step(t, acc):
            u = feature(1, slot, t) * feature(2, slot, t)
            u_s[u_row(slot, t), :] = u
            return tuple(a * d + u for a, d in zip(acc, decay))

        ends = lax.fori_loop(
            REACH,
            STRETCH,
            step,
            tuple(jnp.zeros((8, 128), F32) for _ in range(ORDER)),
            unroll=2,
        )
        largest = jnp.abs(ends[0])
        for end in ends[1:]:
            largest = jnp.maximum(largest, jnp.abs(end))
        scale = jnp.maximum(largest * 1.0078125, TINY).astype(BF16).astype(F32)
        end_scale.append(scale)
        inverse = FULL / scale
        ends = [jnp.round(end * inverse) for end in ends]
        for h in range(2):
            for lg, reg in enumerate(swap_groups(ends[8 * h : 8 * h + 8])):
                stage[pl.ds(lg * 4 + slot * 2 + h, 8, stride=32), :] = reg
    stage_to_send(send_e, 4, 0, code)

    for slot in range(2):
        q_tail = [token(0, slot, 58 + t) for t in range(6)]
        kinds = (
            [token(1, slot, t) for t in range(6)] + q_tail[0:2],
            [token(2, slot, t) for t in range(6)] + [end_scale[slot]] * 2,
            q_tail[4:6] + [token(1, slot, 58 + t) for t in range(6)],
            q_tail[2:4] + [token(2, slot, 58 + t) for t in range(6)],
        )
        for kind in range(4):
            for lg, reg in enumerate(swap_groups(kinds[kind])):
                stage[pl.ds(lg * 8 + slot * 4 + kind, 8, stride=64), :] = reg
    stage_to_send(send_b, 8, 0, narrow)

    pl.semaphore_wait(barrier, OWNERS - 1 + n_ch - 1)
    send_all(send_b, recv_b, 0)
    send_all(send_e, recv_e, 1)
    recv_b[me] = send_b[me]
    recv_e[me] = send_e[me]

    def ones_where(hit):
        return jnp.where(hit, 1.0, 0.0).astype(BF16)

    sos = jnp.broadcast_to(sos_ref[...].astype(F32), (SLOTS, SLOTS)).astype(BF16)
    spread = ones_where(iota((SLOTS, 512), 0) == (iota((SLOTS, 512), 1) >> 2))
    sos4 = jnp.dot(sos[:16], spread, preferred_element_type=F32)
    spread = ones_where(iota((SLOTS, 256), 0) == (iota((SLOTS, 256), 1) >> 1))
    sos2 = jnp.dot(sos[:16], spread, preferred_element_type=F32)
    across = (((1,), (1,)), ((), ()))
    row, lane = iota((512, SLOTS), 0), iota((512, SLOTS), 1)
    part = row & 7
    pair = (row >> 3) * 2
    slot_t = jnp.where(part >= 3, 1, 0)
    slot_s = jnp.where(part < 4, part >> 1, part & 1)
    col_t[...] = lax.dot_general(
        ones_where(lane == pair + slot_t), sos, across, preferred_element_type=F32
    )
    col_s[...] = lax.dot_general(
        ones_where(lane == pair + slot_s), sos, across, preferred_element_type=F32
    )
    lane, sublane = iota((16, 128), 1), iota((16, 128), 0)
    key4 = [
        sos4[:, 128 * c : 128 * c + 128].astype(jnp.int32) * 4 + (lane & 3) for c in range(4)
    ]
    key2 = [
        sos2[:, 128 * c : 128 * c + 128].astype(jnp.int32) * 2 + (lane & 1) for c in range(2)
    ]

    @pl.loop(0, 32)
    def _(b):
        rows = pl.ds(pl.multiple_of(b * 16, 16), 16)
        row = sublane + b * 16
        kind, s = row >> 7, row & 127
        want_b = (s - (kind >> 1)) * 4 + kind
        part = row & 7
        turn = jnp.where(part >= 3, part - 3, part)
        kind = jnp.where(turn > 0, turn + 1, turn)
        want_t = (col_t[rows, :].astype(jnp.int32) - 1) * 4 + kind
        want_t = jnp.where(part < 6, want_t, -1)
        before = col_s[rows, :].astype(jnp.int32) - 1
        want_s = before + jnp.where(part < 4, (part & 1) * 128, 256)
        want_s = jnp.where((part < 6) & (before >= 0), want_s, -1)
        for c in range(4):
            lanes = slice(128 * c, 128 * c + 128)
            pb[rows, lanes] = ones_where(key4[c] == want_b)
            qt[rows, lanes] = ones_where(key4[c] == want_t)
            if c < 3:
                qs[rows, lanes] = ones_where(lane + 128 * c == want_s)

    @pl.loop(0, 16)
    def _(b):
        rows = pl.ds(pl.multiple_of(b * 16, 16), 16)
        row = sublane + b * 16
        want = (row & 127) * 2 + (row >> 7)
        for c in range(2):
            pe[rows, 128 * c : 128 * c + 128] = ones_where(key2[c] == want)

    def own_modes(table):
        found = []
        for h in range(2):
            for lg, reg in enumerate(swap_groups([row8(table, 8 * h + m) for m in range(8)])):
                own[lg * 8 : lg * 8 + 8, :] = reg
            found.append(own[pl.ds(my_lg * 8 + my_sub, 1), :])
        return found

    own_rates, own_amounts = own_modes(rt), own_modes(am)

    lane128 = iota((8, 128), 1)

    def own_taps(array):
        rows = sw[pl.ds(array * 64 + my_sub, 8, stride=8), :]
        rows = pltpu.roll(rows, (128 - GROUP * my_lg) % 128, 1)
        rows = jnp.where(lane128 < GROUP, rows, 0.0)
        for shift in (16, 32, 64):
            rows = rows + pltpu.roll(rows, shift, 1)
        return rows

    taps_k, taps_v = own_taps(1), own_taps(2)
    r_row, r_lane = iota((128, 128), 0), iota((128, 128), 1)
    same = (r_row % GROUP == r_lane % GROUP) & (r_row // GROUP < REACH)
    ago = (STRETCH - 1 - r_row // GROUP).astype(F32)
    for h in range(2):
        mm[:, 128 * h : 128 * h + 128] = jnp.where(same, jnp.exp(-own_rates[h] * ago), 0.0)

    filt[0 : PAD * 8, :] = jnp.zeros((PAD * 8, 128), F32)

    def filter_step(d, powers):
        sums = list(powers)
        while len(sums) > 1:
            sums = [x + y for x, y in zip(sums[0::2], sums[1::2])]
        filt[pl.ds(pl.multiple_of((d + PAD) * 8, 8), 8), :] = sums[0]
        return tuple(p * x for p, x in zip(powers, decay))

    lax.fori_loop(
        0, STRETCH, filter_step, tuple(row8(am, m) for m in range(ORDER)), unroll=2
    )
    filt[PAD * 8 : PAD * 8 + 8, :] = filt[PAD * 8 : PAD * 8 + 8, :] + skip_ref[...]

    for slot in range(2):

        @pl.loop(REACH, STRETCH, unroll=2)
        def _(t):
            z_s[u_row(slot, t), :] = feature(0, slot, t)

    all_of(send_b, recv_b, 0).wait_recv()
    recv_to_stage(recv_b, 8, 0, widen)
    raw = stage[...].astype(BF16)
    stage[...] = jnp.dot(qt[...], raw, preferred_element_type=F32)
    stage_to_send(send_t, 8, 0, narrow)
    send_all(send_t, recv_t, 2)
    recv_t[me] = send_t[me]
    stage[...] = jnp.dot(pb[...], raw, preferred_element_type=F32)
    group16 = iota((16, 128), 1) // GROUP

    @pl.loop(0, 8)
    def _(b):
        def edge(kind, taps):
            head = stage[pl.ds(pl.multiple_of(kind * 128 + b * 16, 16), 16), :]
            tail = stage[pl.ds(pl.multiple_of(kind * 128 + 256 + b * 16, 16), 16), :]
            total = taps[0:1] * head
            for j in range(1, TAPS):
                mixed = jnp.where(group16 < 8 - j, head, tail)
                total = total + taps[j : j + 1] * pltpu.roll(mixed, GROUP * j, 1)
            return total

        rows = pl.ds(pl.multiple_of(b * 16, 16), 16)
        six[rows, :] = edge(0, taps_k) * edge(1, taps_v)
        scale = stage[pl.ds(pl.multiple_of(128 + b * 16, 16), 16), :] * (1.0 / FULL)
        scale = jnp.where(group16 == 6, scale, 0.0)
        for shift in (16, 32, 64):
            scale = scale + pltpu.roll(scale, shift, 1)
        scale_s[rows, :] = scale

    extra = jnp.dot(six[...], mm[...], precision=HIGHEST, preferred_element_type=F32)

    def halves(x):
        hi = jnp.floor(x * (1.0 / 256.0))
        return hi, x - 256.0 * hi

    all_of(send_e, recv_e, 1).wait_recv()
    recv_to_stage(recv_e, 4, 0, uncode)
    hi, lo = halves(stage[0:256, :])
    both = jnp.concatenate([hi.astype(BF16), lo.astype(BF16)], axis=1)
    both = jnp.dot(pe[...], both, preferred_element_type=F32)
    codes = both[:, :128] * 256.0 + both[:, 128:]
    sub8 = iota((8, 128), 0)
    states = []
    for h in range(2):
        x = codes[128 * h : 128 * h + 128] * scale_s[...] + extra[:, 128 * h : 128 * h + 128]
        span = own_rates[h] * float(STRETCH)
        blocks = [x[8 * b : 8 * b + 8] for b in range(16)]
        for d in (1, 2, 4):
            mult = jnp.where(sub8 >= d, jnp.exp(-span * float(d)), 0.0)
            blocks = [x + mult * pltpu.roll(x, d, 0) for x in blocks]
        lift = jnp.exp(-span * (sub8 + 1).astype(F32))
        whole = jnp.broadcast_to(jnp.exp(-span * 8.0), (8, 128))
        carry = jnp.zeros((8, 128), F32)
        done = []
        for b in range(16):
            total = jnp.broadcast_to(blocks[b][7:8], (8, 128))
            done.append((blocks[b] + lift * carry) * own_amounts[h])
            carry = whole * carry + total
        states.append(done)
    for b in range(16):
        x0, x1 = states[0][b], states[1][b]
        largest = jnp.maximum(jnp.abs(x0), jnp.abs(x1))
        for shift in (16, 32, 64):
            largest = jnp.maximum(largest, pltpu.roll(largest, shift, 1))
        power = jnp.ceil(jnp.log2(jnp.maximum(largest, TINY)))
        inverse = jnp.exp2(-power) * FULL
        for h, x in enumerate((x0, x1)):
            hi, lo = halves(jnp.round(x * inverse))
            scan_s[128 * h + 8 * b : 128 * h + 8 * b + 8, 0:128] = hi
            scan_s[128 * h + 8 * b : 128 * h + 8 * b + 8, 128:256] = lo
        scan_s[256 + 8 * b : 256 + 8 * b + 8, 0:128] = jnp.zeros((8, 128), F32)
        scan_s[256 + 8 * b : 256 + 8 * b + 8, 128:256] = power
    both = jnp.dot(qs[...], scan_s[...].astype(BF16), preferred_element_type=F32)
    stage[...] = both[:, :128] * 256.0 + both[:, 128:]
    stage_to_send(send_s, 8, 0, code)
    stage_to_send(send_x, 8, 4, code)
    send_all(send_s, recv_s, 3)
    send_all(send_x, recv_x, 5)
    recv_s[me] = send_s[me]
    recv_x[me] = send_x[me]

    for b in range(8):
        t0 = b * 8

        def inner(s, acc):
            taps = [row8(filt, t0 + i - s + PAD) for i in range(8)]
            out = []
            for slot in range(2):
                u = u_s[u_row(slot, s), :]
                out += [acc[slot * 8 + i] + taps[i] * u for i in range(8)]
            return tuple(out)

        acc = lax.fori_loop(
            REACH,
            t0 + 8,
            inner,
            tuple(jnp.zeros((8, 128), F32) for _ in range(16)),
            unroll=2,
        )
        for slot in range(2):
            for i in range(8):
                y_s[u_row(slot, t0 + i), :] = acc[slot * 8 + i]

    all_of(send_t, recv_t, 2).wait_recv()
    recv_to_stage(recv_t, 8, 0, widen)
    for slot in range(2):
        kinds = [
            swap_groups(
                [stage[pl.ds(lg * 8 + slot * 3 + turn, 8, stride=64), :] for lg in range(8)]
            )
            for turn in range(3)
        ]
        tails = (
            kinds[0][6:8] + kinds[2][0:2] + kinds[1][0:2],
            kinds[1][2:8],
            kinds[2][2:8],
        )
        for array in range(3):
            for t in range(6):
                base = (slot * EXT + t) * 8
                ext[array, base : base + 8, :] = tails[array][t]

    for slot in range(2):
        first = []
        for t in range(REACH):
            first.append(feature(1, slot, t) * feature(2, slot, t))
            z_s[u_row(slot, t), :] = feature(0, slot, t)

        @pl.loop(0, STRETCH, unroll=2)
        def _(t):
            rows = u_row(slot, t)
            total = y_s[rows, :]
            for s in range(REACH):
                total = total + row8(filt, t - s + PAD) * first[s]
            y_s[rows, :] = total

    all_of(send_s, recv_s, 3).wait_recv()
    recv_to_stage(recv_s, 8, 0, uncode)
    all_of(send_x, recv_x, 5).wait_recv()
    recv_to_stage(recv_x, 8, 4, uncode)
    for slot in range(2):
        scales = [
            jnp.exp2(stage[pl.ds(lg * 8 + 4 + slot, 8, stride=64), :]) * (1.0 / FULL)
            for lg in range(8)
        ]
        starts = []
        for h in range(2):
            starts += swap_groups(
                [
                    stage[pl.ds(lg * 8 + slot * 2 + h, 8, stride=64), :] * scales[lg]
                    for lg in range(8)
                ]
            )

        def last(t, state):
            state = tuple(x * d for x, d in zip(state, decay))
            sums = list(state)
            while len(sums) > 1:
                sums = [x + y for x, y in zip(sums[0::2], sums[1::2])]
            rows = u_row(slot, t)
            z_s[rows, :] = z_s[rows, :] * (y_s[rows, :] + sums[0])
            return state

        lax.fori_loop(0, STRETCH, last, tuple(starts), unroll=2)

    @pl.loop(0, 16)
    def _(b):
        rows = pl.ds(pl.multiple_of(b * 8, 8), 8)
        total = jnp.zeros((8, 128), F32)
        for j in range(8):
            z = z_s[pl.ds(b * 64 + j, 8, stride=8), :]
            zn_s[rows, 128 * j : 128 * j + 128] = z
            total = total + z * z
        sq_s[rows, :] = total

    sums = lax.dot_general(
        jnp.ones((8, 128), F32),
        sq_s[...],
        (((1,), (1,)), ((), ())),
        precision=HIGHEST,
        preferred_element_type=F32,
    )
    sq_send[0] = sums
    sq_recv[my_ch] = sums

    @pl.loop(1, n_ch)
    def _(i):
        pltpu.make_async_remote_copy(
            src_ref=sq_send.at[0],
            dst_ref=sq_recv.at[my_ch],
            send_sem=ssem.at[4],
            recv_sem=rsem.at[4],
            device_id={"ch": (my_ch + i) % n_ch},
            device_id_type=MESH,
        ).start()

    every = pltpu.make_async_remote_copy(
        src_ref=sq_recv.at[pl.ds(0, n_ch - 1)],
        dst_ref=sq_recv.at[pl.ds(0, n_ch - 1)],
        send_sem=ssem.at[4],
        recv_sem=rsem.at[4],
        device_id={"ch": (my_ch + 1) % n_ch},
        device_id_type=MESH,
    )
    every.wait_recv()
    total = sq_recv[0]
    for i in range(1, n_ch):
        total = total + sq_recv[i]
    scale = lax.rsqrt(total / float(width_all) + EPS)
    sq_s[...] = jnp.transpose(jnp.broadcast_to(scale[0:1], (128, 128)))

    @pl.loop(0, 8)
    def _(b):
        rows = pl.ds(pl.multiple_of(b * 16, 16), 16)
        by = sq_s[rows, :]
        for j in range(8):
            lanes = slice(128 * j, 128 * j + 128)
            o_ref[rows, lanes] = (zn_s[rows, lanes] * by * gain_ref[:, lanes]).astype(BF16)

    all_of(send_b, recv_b, 0).wait_send()
    all_of(send_e, recv_e, 1).wait_send()
    all_of(send_t, recv_t, 2).wait_send()
    all_of(send_s, recv_s, 3).wait_send()
    all_of(send_x, recv_x, 5).wait_send()
    every.wait_send()


def on_device(n_ch, width_all, q_in, k_in, v_in, stretch_of_slot, short_weight, rates, residues, skip, gain):
    vmem = pl.BlockSpec(memory_space=pltpu.VMEM)
    hbm = pl.BlockSpec(memory_space=pltpu.HBM)
    f32 = lambda *shape: pltpu.VMEM(shape, F32)
    bf16 = lambda *shape: pltpu.VMEM(shape, BF16)
    i16 = lambda *shape: pltpu.VMEM(shape, jnp.int16)
    scratch = (
        [bf16(TOKENS, WIDTH)] * 3
        + [pltpu.VMEM((1, SLOTS), jnp.int32), f32(3, TAPS, WIDTH)]
        + [f32(ORDER, WIDTH)] * 2
        + [f32(8, 128), f32(1, WIDTH)]
        + [f32(3, 2 * EXT * 8, 128)]
        + [f32(TOKENS * 8, 128)] * 3
        + [f32(TOKENS, WIDTH)]
        + [f32(ORDER * 8, 128)] * 2
        + [f32(192, 128), f32((STRETCH + PAD) * 8, 128), f32(512, 128), f32(64, 128), f32(128, 128)]
        + [bf16(512, 512), bf16(512, 512), bf16(256, 256), bf16(512, 384)]
        + [f32(128, 256), f32(384, 256), f32(128, 128), f32(512, 128), f32(512, 128), f32(128, 128)]
        + [bf16(OWNERS, 8, 128)] * 4
        + [i16(OWNERS, 4, 128)] * 4
        + [i16(OWNERS, 2, 128)] * 2
        + [f32(1, 8, 128), f32(n_ch, 8, 128)]
        + [pltpu.SemaphoreType.DMA((6,)), pltpu.SemaphoreType.DMA((6,))]
        + [pltpu.SemaphoreType.DMA((9,))]
    )
    return pl.pallas_call(
        functools.partial(kernel, n_ch, width_all),
        out_shape=jax.ShapeDtypeStruct((TOKENS, WIDTH), BF16),
        in_specs=[hbm] * 9,
        out_specs=vmem,
        scratch_shapes=scratch,
        compiler_params=pltpu.CompilerParams(collective_id=0, has_side_effects=True),
        name="hyena",
    )(
        q_in,
        k_in,
        v_in,
        stretch_of_slot.reshape(1, SLOTS),
        short_weight,
        rates,
        residues,
        skip.reshape(8, 128),
        gain.reshape(1, WIDTH),
    )


def solution(mesh):
    n_ch = mesh.shape["ch"]

    def body(*args):
        return on_device(n_ch, n_ch * WIDTH, *args)

    in_specs = (
        P("ctx", "ch"),
        P("ctx", "ch"),
        P("ctx", "ch"),
        P(),
        P(None, None, "ch"),
        P(None, "ch"),
        P(None, "ch"),
        P("ch"),
        P("ch"),
    )
    return jax.shard_map(
        body, mesh=mesh, in_specs=in_specs, out_specs=P("ctx", "ch"), check_vma=False
    )
```

```python
import functools

import jax
import jax.numpy as jnp
from jax import lax
from jax.experimental import pallas as pl
from jax.experimental.pallas import tpu as pltpu
from jax.sharding import PartitionSpec as P

F32 = jnp.float32
BF16 = jnp.bfloat16
MESH = pl.DeviceIdType.MESH
HIGHEST = lax.Precision.HIGHEST

TOKENS = 128
WIDTH = 1024
STRETCH = 64
REACH = 6
TAPS = 7
ORDER = 16
OWNERS = 64
GROUP = 16
SLOTS = 128
PAD = 8
EPS = 1e-05
FULL = 32000.0
TINY = 1e-30


def iota(shape, dim):
    return lax.broadcasted_iota(jnp.int32, shape, dim)


def swap_groups(regs):
    regs = list(regs)
    group = iota((8, 128), 1) // GROUP
    for bit in (1, 2, 4):
        low = (group & bit) == 0
        for i in range(8):
            if i & bit:
                continue
            x, y = regs[i], regs[i | bit]
            regs[i] = jnp.where(low, x, pltpu.roll(y, GROUP * bit, 1))
            regs[i | bit] = jnp.where(low, pltpu.roll(x, 128 - GROUP * bit, 1), y)
    return regs


def one_minus_exp_neg(x):
    series = 1.0 - x / 9.0
    for n in (8, 7, 6, 5, 4, 3, 2):
        series = 1.0 - (x / n) * series
    return jnp.where(x < 0.3, x * series, 1.0 - jnp.exp(-x))


def kernel(
    n_ch,
    width_all,
    q_hbm,
    k_hbm,
    v_hbm,
    sos_hbm,
    sw_hbm,
    rates_hbm,
    res_hbm,
    skip_hbm,
    gain_hbm,
    o_ref,
    q_ref,
    k_ref,
    v_ref,
    sos_ref,
    sw_ref,
    rates_ref,
    res_ref,
    skip_ref,
    gain_ref,
    ext,
    u_s,
    y_s,
    z_s,
    zn_s,
    rt,
    am,
    sw,
    filt,
    stage,
    own,
    six,
    pb,
    pe,
    qs,
    mm,
    m1,
    extra,
    rows_s,
    codes_s,
    scan_s,
    scale_s,
    col_s,
    sq_s,
    send_b,
    recv_b,
    send_e,
    recv_e,
    send_s,
    recv_s,
    sq_send,
    sq_recv,
    ssem,
    rsem,
    isem,
):
    me = lax.axis_index("ctx")
    my_ch = lax.axis_index("ch")
    my_z, my_l = me // 4, me % 4
    my_sub, my_lg = me // 8, me % 8

    barrier = pltpu.get_barrier_semaphore()

    @pl.loop(1, OWNERS)
    def _(i):
        pl.semaphore_signal(
            barrier, 1, device_id={"ctx": (me + i) % OWNERS}, device_id_type=MESH
        )

    @pl.loop(1, n_ch)
    def _(i):
        pl.semaphore_signal(
            barrier, 1, device_id={"ch": (my_ch + i) % n_ch}, device_id_type=MESH
        )

    def load(i, src, dst):
        copy = pltpu.make_async_copy(src, dst, isem.at[i])
        copy.start()
        return copy

    loads = {
        "rates": load(0, rates_hbm, rates_ref),
        "res": load(1, res_hbm, res_ref),
        "sw": load(2, sw_hbm, sw_ref),
        "k": load(3, k_hbm, k_ref),
        "v": load(4, v_hbm, v_ref),
        "q": load(5, q_hbm, q_ref),
        "sos": load(6, sos_hbm, sos_ref),
        "skip": load(7, skip_hbm, skip_ref),
        "gain": load(8, gain_hbm, gain_ref),
    }

    def send_all(src, dst, sem):
        def one(d):
            pltpu.make_async_remote_copy(
                src_ref=src.at[d],
                dst_ref=dst.at[me],
                send_sem=ssem.at[sem],
                recv_sem=rsem.at[sem],
                device_id={"ctx": d},
                device_id_type=MESH,
            ).start()

        @pl.loop(0, 15)
        def _(i):
            step = 15 - i
            far = (step + 1) // 2
            d_z = (my_z + (2 * (step % 2) - 1) * far + 16) % 16
            for l in range(4):
                one(d_z * 4 + (my_l + l) % 4)

        for l in range(1, 4):
            one(my_z * 4 + (my_l + l) % 4)

    def all_of(src, dst, sem):
        return pltpu.make_async_remote_copy(
            src_ref=src.at[pl.ds(0, OWNERS - 1)],
            dst_ref=dst.at[pl.ds(0, OWNERS - 1)],
            send_sem=ssem.at[sem],
            recv_sem=rsem.at[sem],
            device_id={"ctx": (me + 1) % OWNERS},
            device_id_type=MESH,
        )

    def code(x):
        return x.astype(jnp.int32).astype(jnp.int16)

    def uncode(x):
        return x.astype(jnp.int32).astype(F32)

    def narrow(x):
        return x.astype(BF16)

    def widen(x):
        return x.astype(F32)

    def stage_to_send(dst, pitch, first, convert):
        rows = dst.shape[1]

        @pl.loop(0, 8)
        def _(b):
            for i in range(8):
                d = b * 8 + i
                dst[d] = convert(stage[pl.ds(d * pitch + first, rows), :])

    def recv_to_stage(src, pitch, first, convert):
        rows = src.shape[1]

        @pl.loop(0, 8)
        def _(b):
            for i in range(8):
                d = b * 8 + i
                stage[pl.ds(d * pitch + first, rows), :] = convert(src[d])

    def token(array, slot, t):
        return ext[array, pl.ds(pl.multiple_of((slot * STRETCH + t) * 8, 8), 8), :]

    def row8(ref, i):
        return ref[pl.ds(pl.multiple_of(i * 8, 8), 8), :]

    loads["rates"].wait()
    loads["res"].wait()
    loads["sw"].wait()
    for j in range(8):
        lanes = slice(128 * j, 128 * j + 128)
        rate = rates_ref[:, lanes]
        amount = res_ref[:, lanes] * jnp.sqrt(one_minus_exp_neg(2.0 * rate))
        rt[pl.ds(j, ORDER, stride=8), :] = rate
        am[pl.ds(j, ORDER, stride=8), :] = amount
        for a in range(3):
            sw[pl.ds(a * 64 + j, TAPS, stride=8), :] = sw_ref[a, :, lanes]
    for a in range(3):
        sw[a * 64 + 56 : a * 64 + 64, :] = jnp.zeros((8, 128), F32)

    for array, name, ref in ((1, "k", k_ref), (2, "v", v_ref), (0, "q", q_ref)):
        loads[name].wait()
        for slot in range(2):

            @pl.loop(0, 4)
            def _(tb):
                for j in range(8):
                    rows = ref[
                        pl.ds(pl.multiple_of(slot * STRETCH + tb * 16, 16), 16),
                        128 * j : 128 * j + 128,
                    ].astype(F32)
                    start = (slot * STRETCH + tb * 16) * 8 + j
                    ext[array, pl.ds(start, 16, stride=8), :] = rows
    loads["sos"].wait()
    loads["skip"].wait()
    loads["gain"].wait()

    def feature(array, slot, t):
        total = row8(sw, array * 8) * token(array, slot, t)
        for j in range(1, TAPS):
            total = total + row8(sw, array * 8 + j) * token(array, slot, t - j)
        return total

    def u_row(slot, t):
        return pl.ds(pl.multiple_of((slot * STRETCH + t) * 8, 8), 8)

    decay = [jnp.exp(-row8(rt, m)) for m in range(ORDER)]
    end_scale = []
    for slot in range(2):

        def step(t, acc):
            u = feature(1, slot, t) * feature(2, slot, t)
            u_s[u_row(slot, t), :] = u
            return tuple(a * d + u for a, d in zip(acc, decay))

        ends = lax.fori_loop(
            REACH,
            STRETCH,
            step,
            tuple(jnp.zeros((8, 128), F32) for _ in range(ORDER)),
            unroll=2,
        )
        largest = jnp.abs(ends[0])
        for end in ends[1:]:
            largest = jnp.maximum(largest, jnp.abs(end))
        scale = jnp.maximum(largest * 1.0078125, TINY).astype(BF16).astype(F32)
        end_scale.append(scale)
        inverse = FULL / scale
        ends = [jnp.round(end * inverse) for end in ends]
        for h in range(2):
            for lg, reg in enumerate(swap_groups(ends[8 * h : 8 * h + 8])):
                stage[pl.ds(lg * 4 + slot * 2 + h, 8, stride=32), :] = reg
    stage_to_send(send_e, 4, 0, code)

    for slot in range(2):
        q_tail = [token(0, slot, 58 + t) for t in range(6)]
        kinds = (
            [token(1, slot, t) for t in range(6)] + q_tail[4:6],
            [token(2, slot, t) for t in range(6)] + [end_scale[slot]] * 2,
            q_tail[0:2] + [token(1, slot, 58 + t) for t in range(6)],
            q_tail[2:4] + [token(2, slot, 58 + t) for t in range(6)],
        )
        for kind in range(4):
            for lg, reg in enumerate(swap_groups(kinds[kind])):
                stage[pl.ds(lg * 8 + slot * 4 + kind, 8, stride=64), :] = reg
    stage_to_send(send_b, 8, 0, narrow)

    pl.semaphore_wait(barrier, OWNERS - 1 + n_ch - 1)
    send_all(send_b, recv_b, 0)
    send_all(send_e, recv_e, 1)
    recv_b[me] = send_b[me]
    recv_e[me] = send_e[me]

    def ones_where(hit):
        return jnp.where(hit, 1.0, 0.0).astype(BF16)

    sos = jnp.broadcast_to(sos_ref[...].astype(F32), (SLOTS, SLOTS)).astype(BF16)
    spread = ones_where(iota((SLOTS, 512), 0) == (iota((SLOTS, 512), 1) >> 2))
    sos4 = jnp.dot(sos[:16], spread, preferred_element_type=F32)
    spread = ones_where(iota((SLOTS, 256), 0) == (iota((SLOTS, 256), 1) >> 1))
    sos2 = jnp.dot(sos[:16], spread, preferred_element_type=F32)
    across = (((1,), (1,)), ((), ()))
    spread = ones_where(iota((512, SLOTS), 1) == (iota((512, SLOTS), 0) >> 2))
    col_s[...] = lax.dot_general(spread, sos, across, preferred_element_type=F32)
    lane, sublane = iota((16, 128), 1), iota((16, 128), 0)
    key4 = [
        sos4[:, 128 * c : 128 * c + 128].astype(jnp.int32) * 4 + (lane & 3) for c in range(4)
    ]
    key2 = [
        sos2[:, 128 * c : 128 * c + 128].astype(jnp.int32) * 2 + (lane & 1) for c in range(2)
    ]

    @pl.loop(0, 40)
    def _(b):
        rows = pl.ds(pl.multiple_of(b * 16, 16), 16)
        row = sublane + b * 16
        block = row >> 7
        want = ((row & 127) - jnp.where(block >= 2, 1, 0)) * 4 + (block & 3)
        for c in range(4):
            pb[rows, 128 * c : 128 * c + 128] = ones_where(key4[c] == want)

    @pl.loop(0, 32)
    def _(b):
        rows = pl.ds(pl.multiple_of(b * 16, 16), 16)
        want = (sublane & 3) * 128 + col_s[rows, :].astype(jnp.int32)
        for c in range(4):
            qs[rows, 128 * c : 128 * c + 128] = ones_where(lane + 128 * c == want)

    @pl.loop(0, 16)
    def _(b):
        rows = pl.ds(pl.multiple_of(b * 16, 16), 16)
        row = sublane + b * 16
        want = (row & 127) * 2 + (row >> 7)
        for c in range(2):
            pe[rows, 128 * c : 128 * c + 128] = ones_where(key2[c] == want)

    filt[0 : PAD * 8, :] = jnp.zeros((PAD * 8, 128), F32)

    def filter_step(d, powers):
        sums = list(powers)
        while len(sums) > 1:
            sums = [x + y for x, y in zip(sums[0::2], sums[1::2])]
        filt[pl.ds(pl.multiple_of((d + PAD) * 8, 8), 8), :] = sums[0]
        return tuple(p * x for p, x in zip(powers, decay))

    lax.fori_loop(
        0, STRETCH, filter_step, tuple(row8(am, m) for m in range(ORDER)), unroll=2
    )
    filt[PAD * 8 : PAD * 8 + 8, :] = filt[PAD * 8 : PAD * 8 + 8, :] + skip_ref[...]

    for slot in range(2):

        for t in range(REACH):
            total = row8(sw, 0) * token(0, slot, t)
            for j in range(1, t + 1):
                total = total + row8(sw, j) * token(0, slot, t - j)
            z_s[u_row(slot, t), :] = total

        @pl.loop(REACH, STRETCH, unroll=2)
        def _(t):
            z_s[u_row(slot, t), :] = feature(0, slot, t)

    def own_modes(table):
        found = []
        for h in range(2):
            for lg, reg in enumerate(swap_groups([row8(table, 8 * h + m) for m in range(8)])):
                own[lg * 8 : lg * 8 + 8, :] = reg
            found.append(own[pl.ds(my_lg * 8 + my_sub, 1), :])
        return found

    own_rates, own_amounts = own_modes(rt), own_modes(am)

    lane128 = iota((8, 128), 1)

    def own_taps(table, first):
        rows = table[pl.ds(first + my_sub, 8, stride=8), :]
        rows = pltpu.roll(rows, (128 - GROUP * my_lg) % 128, 1)
        rows = jnp.where(lane128 < GROUP, rows, 0.0)
        for shift in (16, 32, 64):
            rows = rows + pltpu.roll(rows, shift, 1)
        return rows

    taps_q, taps_k, taps_v = own_taps(sw, 0), own_taps(sw, 64), own_taps(sw, 128)
    own_filter = own_taps(filt, PAD * 8)
    r_row, r_lane = iota((128, 128), 0), iota((128, 128), 1)
    same = (r_row & (GROUP - 1)) == (r_lane & (GROUP - 1))
    g_row, g_lane = r_row >> 4, r_lane >> 4
    inside = same & (g_row < REACH)
    for h in range(2):
        lift = jnp.exp(-own_rates[h] * (REACH - 1 - g_row).astype(F32))
        mm[:, 128 * h : 128 * h + 128] = jnp.where(inside, lift, 0.0)
        rate = jnp.transpose(jnp.broadcast_to(own_rates[h], (128, 128)))
        lift = jnp.exp(-rate * (g_lane + 1).astype(F32))
        lift = jnp.where(same & (g_lane < REACH), lift, 0.0)
        upper = lift.astype(BF16)
        lower = (lift - upper.astype(F32)).astype(BF16)
        for i, part in enumerate((upper, lower, upper)):
            m1[256 * i + 128 * h : 256 * i + 128 * h + 128, :] = part
    near = jnp.zeros((128, 128), F32)
    inside = inside & (g_lane < REACH)
    for d in range(REACH):
        near = jnp.where(inside & (g_lane - g_row == d), own_filter[d : d + 1], near)
    mm[:, 256:384] = near

    def halves(x):
        hi = jnp.floor(x * (1.0 / 256.0))
        return hi, x - 256.0 * hi

    def group_max(x):
        for shift in (16, 32, 64):
            x = jnp.maximum(x, pltpu.roll(x, shift, 1))
        return x

    def power_of(largest):
        return jnp.ceil(jnp.log2(jnp.maximum(largest, TINY)))

    def encode(x, power):
        return jnp.round(x * (jnp.exp2(-power) * FULL))

    def put(kind, rows, x):
        hi, lo = halves(x)
        at = pl.ds(kind * 128 + rows, x.shape[0])
        codes_s[at, 0:128] = hi.astype(BF16)
        codes_s[at, 128:256] = lo.astype(BF16)

    all_of(send_b, recv_b, 0).wait_recv()
    recv_to_stage(recv_b, 8, 0, widen)
    rows_s[...] = jnp.dot(pb[...], stage[...].astype(BF16), preferred_element_type=F32)
    group = iota((16, 128), 1) >> 4

    @pl.loop(0, 8)
    def _(b):
        first = pl.multiple_of(b * 16, 16)

        def block(kind):
            return rows_s[pl.ds(pl.multiple_of(kind * 128 + b * 16, 16), 16), :]

        def edge(head, tail, taps):
            total = taps[0:1] * head
            for j in range(1, TAPS):
                mixed = jnp.where(group < 8 - j, head, tail)
                total = total + taps[j : j + 1] * pltpu.roll(mixed, GROUP * j, 1)
            return total

        rows = pl.ds(first, 16)
        head_v, tail_k, tail_v = block(1), block(2), block(3)
        six[rows, :] = edge(block(0), tail_k, taps_k) * edge(head_v, tail_v, taps_v)
        scale = jnp.where(group == 6, head_v * (1.0 / FULL), 0.0)
        for shift in (16, 32, 64):
            scale = scale + pltpu.roll(scale, shift, 1)
        scale_s[rows, :] = scale
        tail_q = jnp.where(group >= 4, pltpu.roll(tail_v, 64, 1), pltpu.roll(tail_k, 32, 1))
        tail_q = jnp.where(group >= 6, block(4), tail_q)
        part = edge(jnp.zeros_like(tail_q), tail_q, taps_q)
        part = jnp.where(group < REACH, part, 0.0)
        power = power_of(group_max(jnp.abs(part)))
        put(3, first, jnp.where(group == 6, power, encode(part, power)))

    extra[...] = jnp.dot(six[...], mm[...], precision=HIGHEST, preferred_element_type=F32)

    all_of(send_e, recv_e, 1).wait_recv()
    recv_to_stage(recv_e, 4, 0, uncode)
    hi, lo = halves(stage[0:256, :])
    both = jnp.concatenate([hi.astype(BF16), lo.astype(BF16)], axis=1)
    both = jnp.dot(pe[...], both, preferred_element_type=F32)
    codes = both[:, :128] * 256.0 + both[:, 128:]
    sub8 = iota((8, 128), 0)
    for h in range(2):
        lanes = slice(128 * h, 128 * h + 128)
        late = jnp.exp(-own_rates[h] * float(STRETCH - REACH))
        x = codes[128 * h : 128 * h + 128] * scale_s[...] + extra[:, lanes] * late
        span = own_rates[h] * float(STRETCH)
        blocks = [x[8 * b : 8 * b + 8] for b in range(16)]
        for d in (1, 2, 4):
            mult = jnp.where(sub8 >= d, jnp.exp(-span * float(d)), 0.0)
            blocks = [x + mult * pltpu.roll(x, d, 0) for x in blocks]
        lift = jnp.exp(-span * (sub8 + 1).astype(F32))
        whole = jnp.broadcast_to(jnp.exp(-span * 8.0), (8, 128))
        carry = jnp.zeros((8, 128), F32)
        scan_s[h, 0:8, :] = carry
        for b in range(16):
            total = jnp.broadcast_to(blocks[b][7:8], (8, 128))
            scan_s[h, 8 * b + 1 : 8 * b + 9, :] = blocks[b] + lift * carry
            carry = whole * carry + total
    start = [scan_s[h, 0:128, :] * own_amounts[h] for h in range(2)]
    wide = jnp.concatenate(start, axis=1)
    upper = wide.astype(BF16)
    lower = (wide - upper.astype(F32)).astype(BF16)
    wide = jnp.concatenate([upper, upper, lower], axis=1)
    rows_s[0:128, :] = extra[:, 256:384] + jnp.dot(
        wide, m1[...], preferred_element_type=F32
    )
    late = [
        start[h] * jnp.exp(-own_rates[h] * float(REACH))
        + extra[:, 128 * h : 128 * h + 128] * own_amounts[h]
        for h in range(2)
    ]
    for b in range(8):
        rows = slice(16 * b, 16 * b + 16)
        power = power_of(
            group_max(jnp.maximum(jnp.abs(late[0][rows]), jnp.abs(late[1][rows])))
        )
        for h in range(2):
            put(h, 16 * b, encode(late[h][rows], power))
        y = rows_s[rows, :]
        power_y = power_of(group_max(jnp.abs(y)))
        y = jnp.where(group == 6, power, jnp.where(group == 7, power_y, encode(y, power_y)))
        put(2, 16 * b, y)
    both = jnp.dot(qs[...], codes_s[...], preferred_element_type=F32)
    stage[...] = both[:, :128] * 256.0 + both[:, 128:]
    stage_to_send(send_s, 8, 0, code)
    send_all(send_s, recv_s, 2)
    recv_s[me] = send_s[me]

    for b in range(8):
        t0 = b * 8

        def inner(s, acc):
            taps = [row8(filt, t0 + i - s + PAD) for i in range(8)]
            out = []
            for slot in range(2):
                u = u_s[u_row(slot, s), :]
                out += [acc[slot * 8 + i] + taps[i] * u for i in range(8)]
            return tuple(out)

        acc = lax.fori_loop(
            REACH,
            t0 + 8,
            inner,
            tuple(jnp.zeros((8, 128), F32) for _ in range(16)),
            unroll=2,
        )
        for slot in range(2):
            for i in range(8):
                y_s[u_row(slot, t0 + i), :] = acc[slot * 8 + i]

    all_of(send_s, recv_s, 2).wait_recv()
    recv_to_stage(recv_s, 8, 0, uncode)
    for slot in range(2):
        low, high, y_part, q_part = [
            swap_groups(
                [stage[pl.ds(lg * 8 + slot * 4 + kind, 8, stride=64), :] for lg in range(8)]
            )
            for kind in range(4)
        ]
        scale = jnp.exp2(y_part[6]) * (1.0 / FULL)
        scale_y = jnp.exp2(y_part[7]) * (1.0 / FULL)
        scale_q = jnp.exp2(q_part[6]) * (1.0 / FULL)
        for t in range(REACH):
            rows = u_row(slot, t)
            query = z_s[rows, :] + q_part[t] * scale_q
            z_s[rows, :] = query * (y_part[t] * scale_y)

        def last(t, state):
            state = tuple(x * d for x, d in zip(state, decay))
            sums = list(state)
            while len(sums) > 1:
                sums = [x + y for x, y in zip(sums[0::2], sums[1::2])]
            rows = u_row(slot, t)
            z_s[rows, :] = z_s[rows, :] * (y_s[rows, :] + sums[0])
            return state

        lax.fori_loop(
            REACH, STRETCH, last, tuple(x * scale for x in low + high), unroll=2
        )

    @pl.loop(0, 16)
    def _(b):
        rows = pl.ds(pl.multiple_of(b * 8, 8), 8)
        total = jnp.zeros((8, 128), F32)
        for j in range(8):
            z = z_s[pl.ds(b * 64 + j, 8, stride=8), :]
            zn_s[rows, 128 * j : 128 * j + 128] = z
            total = total + z * z
        sq_s[rows, :] = total

    sums = lax.dot_general(
        jnp.ones((8, 128), F32),
        sq_s[...],
        (((1,), (1,)), ((), ())),
        precision=HIGHEST,
        preferred_element_type=F32,
    )
    sq_send[0] = sums
    sq_recv[my_ch] = sums

    @pl.loop(1, n_ch)
    def _(i):
        pltpu.make_async_remote_copy(
            src_ref=sq_send.at[0],
            dst_ref=sq_recv.at[my_ch],
            send_sem=ssem.at[3],
            recv_sem=rsem.at[3],
            device_id={"ch": (my_ch + i) % n_ch},
            device_id_type=MESH,
        ).start()

    every = pltpu.make_async_remote_copy(
        src_ref=sq_recv.at[pl.ds(0, n_ch - 1)],
        dst_ref=sq_recv.at[pl.ds(0, n_ch - 1)],
        send_sem=ssem.at[3],
        recv_sem=rsem.at[3],
        device_id={"ch": (my_ch + 1) % n_ch},
        device_id_type=MESH,
    )
    every.wait_recv()
    total = sq_recv[0]
    for i in range(1, n_ch):
        total = total + sq_recv[i]
    scale = lax.rsqrt(total / float(width_all) + EPS)
    sq_s[...] = jnp.transpose(jnp.broadcast_to(scale[0:1], (128, 128)))

    @pl.loop(0, 8)
    def _(b):
        rows = pl.ds(pl.multiple_of(b * 16, 16), 16)
        by = sq_s[rows, :]
        for j in range(8):
            lanes = slice(128 * j, 128 * j + 128)
            o_ref[rows, lanes] = (zn_s[rows, lanes] * by * gain_ref[:, lanes]).astype(BF16)

    all_of(send_b, recv_b, 0).wait_send()
    all_of(send_e, recv_e, 1).wait_send()
    all_of(send_s, recv_s, 2).wait_send()
    every.wait_send()


def on_device(n_ch, width_all, q_in, k_in, v_in, stretch_of_slot, short_weight, rates, residues, skip, gain):
    vmem = pl.BlockSpec(memory_space=pltpu.VMEM)
    hbm = pl.BlockSpec(memory_space=pltpu.HBM)
    f32 = lambda *shape: pltpu.VMEM(shape, F32)
    bf16 = lambda *shape: pltpu.VMEM(shape, BF16)
    i16 = lambda *shape: pltpu.VMEM(shape, jnp.int16)
    scratch = (
        [bf16(TOKENS, WIDTH)] * 3
        + [pltpu.VMEM((1, SLOTS), jnp.int32), f32(3, TAPS, WIDTH)]
        + [f32(ORDER, WIDTH)] * 2
        + [f32(8, 128), f32(1, WIDTH)]
        + [f32(3, TOKENS * 8, 128)]
        + [f32(TOKENS * 8, 128)] * 3
        + [f32(TOKENS, WIDTH)]
        + [f32(ORDER * 8, 128)] * 2
        + [f32(192, 128), f32((STRETCH + PAD) * 8, 128), f32(512, 128), f32(64, 128), f32(128, 128)]
        + [bf16(640, 512), bf16(256, 256), bf16(512, 512)]
        + [f32(128, 384), bf16(768, 128), f32(128, 384), f32(640, 128), bf16(512, 256)]
        + [f32(2, 136, 128), f32(128, 128), f32(512, 128), f32(128, 128)]
        + [bf16(OWNERS, 8, 128)] * 2
        + [i16(OWNERS, 4, 128)] * 2
        + [i16(OWNERS, 8, 128)] * 2
        + [f32(1, 8, 128), f32(n_ch, 8, 128)]
        + [pltpu.SemaphoreType.DMA((4,)), pltpu.SemaphoreType.DMA((4,))]
        + [pltpu.SemaphoreType.DMA((9,))]
    )
    return pl.pallas_call(
        functools.partial(kernel, n_ch, width_all),
        out_shape=jax.ShapeDtypeStruct((TOKENS, WIDTH), BF16),
        in_specs=[hbm] * 9,
        out_specs=vmem,
        scratch_shapes=scratch,
        compiler_params=pltpu.CompilerParams(collective_id=0, has_side_effects=True),
        name="hyena",
    )(
        q_in,
        k_in,
        v_in,
        stretch_of_slot.reshape(1, SLOTS),
        short_weight,
        rates,
        residues,
        skip.reshape(8, 128),
        gain.reshape(1, WIDTH),
    )


def solution(mesh):
    n_ch = mesh.shape["ch"]

    def body(*args):
        return on_device(n_ch, n_ch * WIDTH, *args)

    in_specs = (
        P("ctx", "ch"),
        P("ctx", "ch"),
        P("ctx", "ch"),
        P(),
        P(None, None, "ch"),
        P(None, "ch"),
        P(None, "ch"),
        P("ch"),
        P("ch"),
    )
    return jax.shard_map(
        body, mesh=mesh, in_specs=in_specs, out_specs=P("ctx", "ch"), check_vma=False
    )
```

```python
import functools

import jax
import jax.numpy as jnp
from jax import lax
from jax.experimental import pallas as pl
from jax.experimental.pallas import tpu as pltpu
from jax.sharding import PartitionSpec as P

F32 = jnp.float32
BF16 = jnp.bfloat16
MESH = pl.DeviceIdType.MESH
HIGHEST = lax.Precision.HIGHEST

TOKENS = 128
WIDTH = 1024
STRETCH = 64
REACH = 6
TAPS = 7
ORDER = 16
OWNERS = 64
GROUP = 16
SLOTS = 128
PAD = 8
EPS = 1e-05
FULL = 32000.0
TINY = 1e-30


def iota(shape, dim):
    return lax.broadcasted_iota(jnp.int32, shape, dim)


def swap_groups(regs):
    regs = list(regs)
    group = iota((8, 128), 1) // GROUP
    for bit in (1, 2, 4):
        low = (group & bit) == 0
        for i in range(8):
            if i & bit:
                continue
            x, y = regs[i], regs[i | bit]
            regs[i] = jnp.where(low, x, pltpu.roll(y, GROUP * bit, 1))
            regs[i | bit] = jnp.where(low, pltpu.roll(x, 128 - GROUP * bit, 1), y)
    return regs


def one_minus_exp_neg(x):
    series = 1.0 - x / 9.0
    for n in (8, 7, 6, 5, 4, 3, 2):
        series = 1.0 - (x / n) * series
    return jnp.where(x < 0.3, x * series, 1.0 - jnp.exp(-x))


def kernel(
    n_ch,
    width_all,
    q_hbm,
    k_hbm,
    v_hbm,
    sos_hbm,
    sw_hbm,
    rates_hbm,
    res_hbm,
    skip_hbm,
    gain_hbm,
    o_ref,
    q_ref,
    k_ref,
    v_ref,
    sos_ref,
    sw_ref,
    rates_ref,
    res_ref,
    skip_ref,
    gain_ref,
    ext,
    u_s,
    y_s,
    z_s,
    zn_s,
    rt,
    am,
    sw,
    filt,
    stage,
    own,
    six,
    gather,
    scatter,
    powers,
    mm,
    m1,
    extra,
    rows_s,
    codes_s,
    scan_s,
    scale_s,
    sq_s,
    send_b,
    recv_b,
    send_e,
    recv_e,
    send_s,
    recv_s,
    sq_send,
    sq_recv,
    ssem,
    rsem,
    isem,
):
    me = lax.axis_index("ctx")
    my_ch = lax.axis_index("ch")
    my_z, my_l = me // 4, me % 4
    my_sub, my_lg = me // 8, me % 8

    barrier = pltpu.get_barrier_semaphore()

    @pl.loop(1, OWNERS)
    def _(i):
        pl.semaphore_signal(
            barrier, 1, device_id={"ctx": (me + i) % OWNERS}, device_id_type=MESH
        )

    @pl.loop(1, n_ch)
    def _(i):
        pl.semaphore_signal(
            barrier, 1, device_id={"ch": (my_ch + i) % n_ch}, device_id_type=MESH
        )

    def load(i, src, dst):
        copy = pltpu.make_async_copy(src, dst, isem.at[i])
        copy.start()
        return copy

    loads = {
        "rates": load(0, rates_hbm, rates_ref),
        "res": load(1, res_hbm, res_ref),
        "sw": load(2, sw_hbm, sw_ref),
        "k": load(3, k_hbm, k_ref),
        "v": load(4, v_hbm, v_ref),
        "q": load(5, q_hbm, q_ref),
        "sos": load(6, sos_hbm, sos_ref),
        "skip": load(7, skip_hbm, skip_ref),
        "gain": load(8, gain_hbm, gain_ref),
    }

    def send_all(src, dst, sem):
        def one(d):
            pltpu.make_async_remote_copy(
                src_ref=src.at[d],
                dst_ref=dst.at[me],
                send_sem=ssem.at[sem],
                recv_sem=rsem.at[sem],
                device_id={"ctx": d},
                device_id_type=MESH,
            ).start()

        @pl.loop(0, 15)
        def _(i):
            step = 15 - i
            far = (step + 1) // 2
            d_z = (my_z + (2 * (step % 2) - 1) * far + 16) % 16
            for l in range(4):
                one(d_z * 4 + (my_l + l) % 4)

        for l in range(1, 4):
            one(my_z * 4 + (my_l + l) % 4)

    def all_of(src, dst, sem):
        return pltpu.make_async_remote_copy(
            src_ref=src.at[pl.ds(0, OWNERS - 1)],
            dst_ref=dst.at[pl.ds(0, OWNERS - 1)],
            send_sem=ssem.at[sem],
            recv_sem=rsem.at[sem],
            device_id={"ctx": (me + 1) % OWNERS},
            device_id_type=MESH,
        )

    def code(x):
        return x.astype(jnp.int32).astype(jnp.int16)

    def uncode(x):
        return x.astype(jnp.int32).astype(F32)

    def narrow(x):
        return x.astype(BF16)

    def widen(x):
        return x.astype(F32)

    def stage_to_send(dst, pitch, first, convert):
        rows = dst.shape[1]

        @pl.loop(0, 8)
        def _(b):
            for i in range(8):
                d = b * 8 + i
                dst[d] = convert(stage[pl.ds(d * pitch + first, rows), :])

    def recv_to_stage(src, pitch, first, convert):
        rows = src.shape[1]

        @pl.loop(0, 8)
        def _(b):
            for i in range(8):
                d = b * 8 + i
                stage[pl.ds(d * pitch + first, rows), :] = convert(src[d])

    def token(array, slot, t):
        return ext[array, pl.ds(pl.multiple_of((slot * STRETCH + t) * 8, 8), 8), :]

    def row8(ref, i):
        return ref[pl.ds(pl.multiple_of(i * 8, 8), 8), :]

    loads["rates"].wait()
    loads["res"].wait()
    loads["sw"].wait()
    for j in range(8):
        lanes = slice(128 * j, 128 * j + 128)
        rate = rates_ref[:, lanes]
        amount = res_ref[:, lanes] * jnp.sqrt(one_minus_exp_neg(2.0 * rate))
        rt[pl.ds(j, ORDER, stride=8), :] = rate
        am[pl.ds(j, ORDER, stride=8), :] = amount
        for a in range(3):
            sw[pl.ds(a * 64 + j, TAPS, stride=8), :] = sw_ref[a, :, lanes]
    for a in range(3):
        sw[a * 64 + 56 : a * 64 + 64, :] = jnp.zeros((8, 128), F32)

    for array, name, ref in ((1, "k", k_ref), (2, "v", v_ref), (0, "q", q_ref)):
        loads[name].wait()
        for slot in range(2):

            @pl.loop(0, 4)
            def _(tb):
                for j in range(8):
                    rows = ref[
                        pl.ds(pl.multiple_of(slot * STRETCH + tb * 16, 16), 16),
                        128 * j : 128 * j + 128,
                    ].astype(F32)
                    start = (slot * STRETCH + tb * 16) * 8 + j
                    ext[array, pl.ds(start, 16, stride=8), :] = rows
    loads["sos"].wait()
    loads["skip"].wait()
    loads["gain"].wait()

    def feature(array, slot, t):
        total = row8(sw, array * 8) * token(array, slot, t)
        for j in range(1, TAPS):
            total = total + row8(sw, array * 8 + j) * token(array, slot, t - j)
        return total

    def u_row(slot, t):
        return pl.ds(pl.multiple_of((slot * STRETCH + t) * 8, 8), 8)

    decay = [jnp.exp(-row8(rt, m)) for m in range(ORDER)]
    end_scale = []
    for slot in range(2):

        def step(t, acc):
            u = feature(1, slot, t) * feature(2, slot, t)
            u_s[u_row(slot, t), :] = u
            return tuple(a * d + u for a, d in zip(acc, decay))

        ends = lax.fori_loop(
            REACH,
            STRETCH,
            step,
            tuple(jnp.zeros((8, 128), F32) for _ in range(ORDER)),
            unroll=2,
        )
        largest = jnp.abs(ends[0])
        for end in ends[1:]:
            largest = jnp.maximum(largest, jnp.abs(end))
        scale = jnp.maximum(largest * 1.0078125, TINY).astype(BF16).astype(F32)
        end_scale.append(scale)
        inverse = FULL / scale
        ends = [jnp.round(end * inverse) for end in ends]
        for h in range(2):
            for lg, reg in enumerate(swap_groups(ends[8 * h : 8 * h + 8])):
                stage[pl.ds(lg * 4 + slot * 2 + h, 8, stride=32), :] = reg
    stage_to_send(send_e, 4, 0, code)

    for slot in range(2):
        q_tail = [token(0, slot, 58 + t) for t in range(6)]
        kinds = (
            [token(1, slot, t) for t in range(6)] + q_tail[4:6],
            [token(2, slot, t) for t in range(6)] + [end_scale[slot]] * 2,
            q_tail[0:2] + [token(1, slot, 58 + t) for t in range(6)],
            q_tail[2:4] + [token(2, slot, 58 + t) for t in range(6)],
        )
        for kind in range(4):
            for lg, reg in enumerate(swap_groups(kinds[kind])):
                stage[pl.ds(lg * 8 + slot * 4 + kind, 8, stride=64), :] = reg
    stage_to_send(send_b, 8, 0, narrow)

    pl.semaphore_wait(barrier, OWNERS - 1 + n_ch - 1)
    send_all(send_b, recv_b, 0)
    send_all(send_e, recv_e, 1)
    recv_b[me] = send_b[me]
    recv_e[me] = send_e[me]

    def ones_where(hit):
        return jnp.where(hit, 1.0, 0.0).astype(BF16)

    sos_row = jnp.broadcast_to(sos_ref[...], (16, SLOTS))
    sublane = iota((16, SLOTS), 0)
    for b in range(16):
        s = sublane + (16 * b - (129 if b >= 8 else 0))
        gather[16 * b : 16 * b + 16, :] = ones_where(sos_row == s)
    sos_column = jnp.transpose(jnp.broadcast_to(sos_ref[...].astype(F32), (SLOTS, SLOTS)))
    scatter[...] = ones_where(sos_column.astype(jnp.int32) == iota((SLOTS, SLOTS), 1))

    filt[0 : PAD * 8, :] = jnp.zeros((PAD * 8, 128), F32)

    def filter_step(d, powers):
        sums = list(powers)
        while len(sums) > 1:
            sums = [x + y for x, y in zip(sums[0::2], sums[1::2])]
        filt[pl.ds(pl.multiple_of((d + PAD) * 8, 8), 8), :] = sums[0]
        return tuple(p * x for p, x in zip(powers, decay))

    lax.fori_loop(
        0, STRETCH, filter_step, tuple(row8(am, m) for m in range(ORDER)), unroll=2
    )
    filt[PAD * 8 : PAD * 8 + 8, :] = filt[PAD * 8 : PAD * 8 + 8, :] + skip_ref[...]

    for slot in range(2):

        for t in range(REACH):
            total = row8(sw, 0) * token(0, slot, t)
            for j in range(1, t + 1):
                total = total + row8(sw, j) * token(0, slot, t - j)
            z_s[u_row(slot, t), :] = total

        @pl.loop(REACH, STRETCH, unroll=2)
        def _(t):
            z_s[u_row(slot, t), :] = feature(0, slot, t)

    def own_modes(table):
        found = []
        for h in range(2):
            for lg, reg in enumerate(swap_groups([row8(table, 8 * h + m) for m in range(8)])):
                own[lg * 8 : lg * 8 + 8, :] = reg
            found.append(own[pl.ds(my_lg * 8 + my_sub, 1), :])
        return found

    own_rates, own_amounts = own_modes(rt), own_modes(am)

    lane128 = iota((8, 128), 1)

    def own_taps(table, first):
        rows = table[pl.ds(first + my_sub, 8, stride=8), :]
        rows = pltpu.roll(rows, (128 - GROUP * my_lg) % 128, 1)
        rows = jnp.where(lane128 < GROUP, rows, 0.0)
        for shift in (16, 32, 64):
            rows = rows + pltpu.roll(rows, shift, 1)
        return rows

    taps_q, taps_k, taps_v = own_taps(sw, 0), own_taps(sw, 64), own_taps(sw, 128)
    own_filter = own_taps(filt, PAD * 8)
    r_row, r_lane = iota((128, 128), 0), iota((128, 128), 1)
    same = (r_row & (GROUP - 1)) == (r_lane & (GROUP - 1))
    g_row, g_lane = r_row >> 4, r_lane >> 4
    inside = same & (g_row < REACH)

    def split(x):
        upper = x.astype(BF16)
        return upper, (x - upper.astype(F32)).astype(BF16)

    def put_mm(part, x):
        lanes = slice(128 * part, 128 * part + 128)
        mm[0:128, lanes], mm[128:256, lanes] = split(x)
        mm[256:384, lanes] = mm[0:128, lanes]

    for h in range(2):
        lift = jnp.exp(-own_rates[h] * (REACH - 1 - g_row).astype(F32))
        put_mm(h, jnp.where(inside, lift, 0.0))
        rate = jnp.transpose(jnp.broadcast_to(own_rates[h], (128, 128)))
        lift = jnp.exp(-rate * (g_lane + 1).astype(F32))
        lift = jnp.where(same & (g_lane < REACH), lift, 0.0)
        upper, lower = split(lift)
        for i, part in enumerate((upper, lower, upper)):
            m1[256 * i + 128 * h : 256 * i + 128 * h + 128, :] = part
    near = jnp.zeros((128, 128), F32)
    inside = inside & (g_lane < REACH)
    for d in range(REACH):
        near = jnp.where(inside & (g_lane - g_row == d), own_filter[d : d + 1], near)
    put_mm(2, near)
    sub8 = iota((8, 128), 0)
    for h in range(2):
        span = own_rates[h] * float(STRETCH)
        for i, d in enumerate((1, 2, 4)):
            powers[h, 8 * i : 8 * i + 8, :] = jnp.where(sub8 >= d, jnp.exp(-span * float(d)), 0.0)
        powers[h, 24:32, :] = jnp.exp(-span * (sub8 + 1).astype(F32))
        powers[h, 32:40, :] = jnp.broadcast_to(jnp.exp(-span * 8.0), (8, 128))
        powers[h, 40:41, :] = jnp.exp(-own_rates[h] * float(STRETCH - REACH))
        powers[h, 41:42, :] = jnp.exp(-own_rates[h] * float(REACH))
        powers[h, 42:43, :] = own_amounts[h]

    def halves(x):
        hi = jnp.floor(x * (1.0 / 256.0))
        return hi, x - 256.0 * hi

    def group_max(x):
        for shift in (16, 32, 64):
            x = jnp.maximum(x, pltpu.roll(x, shift, 1))
        return x

    def power_of(largest):
        return jnp.ceil(jnp.log2(jnp.maximum(largest, TINY)))

    def encode(x, power):
        return jnp.round(x * (jnp.exp2(-power) * FULL))

    def put(kind, rows, x):
        hi, lo = halves(x)
        at = pl.ds(rows, x.shape[0])
        codes_s[at, kind * 256 : kind * 256 + 128] = hi.astype(BF16)
        codes_s[at, kind * 256 + 128 : kind * 256 + 256] = lo.astype(BF16)

    all_of(send_b, recv_b, 0).wait_recv()
    recv_to_stage(recv_b, 8, 0, widen)
    raw = jnp.concatenate(
        [stage[pl.ds(kind, SLOTS, stride=4), :].astype(BF16) for kind in range(4)], axis=1
    )
    rows_s[0:128, 0:256] = jnp.dot(gather[0:128, :], raw[:, 0:256], preferred_element_type=F32)
    rows_s[128:256, :] = jnp.dot(gather[128:256, :], raw, preferred_element_type=F32)
    group = iota((16, 128), 1) >> 4

    @pl.loop(0, 8, unroll=2)
    def _(b):
        first = pl.multiple_of(b * 16, 16)

        def block(kind, before):
            at = pl.ds(pl.multiple_of(before * 128 + b * 16, 16), 16)
            return rows_s[at, kind * 128 : kind * 128 + 128]

        def edge(head, tail, taps):
            total = taps[0:1] * head
            for j in range(1, TAPS):
                mixed = jnp.where(group < 8 - j, head, tail)
                total = total + taps[j : j + 1] * pltpu.roll(mixed, GROUP * j, 1)
            return total

        rows = pl.ds(first, 16)
        head_v, tail_k, tail_v = block(1, 0), block(2, 1), block(3, 1)
        six[rows, :] = edge(block(0, 0), tail_k, taps_k) * edge(head_v, tail_v, taps_v)
        scale = jnp.where(group == 6, head_v * (1.0 / FULL), 0.0)
        for shift in (16, 32, 64):
            scale = scale + pltpu.roll(scale, shift, 1)
        scale_s[rows, :] = scale
        tail_q = jnp.where(group >= 4, pltpu.roll(tail_v, 64, 1), pltpu.roll(tail_k, 32, 1))
        tail_q = jnp.where(group >= 6, block(0, 1), tail_q)
        part = edge(jnp.zeros_like(tail_q), tail_q, taps_q)
        part = jnp.where(group < REACH, part, 0.0)
        power = power_of(group_max(jnp.abs(part)))
        put(3, first, jnp.where(group == 6, power, encode(part, power)))

    upper, lower = split(six[...])
    wide = jnp.concatenate([upper, upper, lower], axis=1)
    extra[...] = jnp.dot(wide, mm[...], preferred_element_type=F32)

    all_of(send_e, recv_e, 1).wait_recv()
    recv_to_stage(recv_e, 4, 0, uncode)
    parts = []
    for h in range(2):
        parts += [x.astype(BF16) for x in halves(stage[pl.ds(h, SLOTS, stride=2), :])]
    both = jnp.concatenate(parts, axis=1)
    both = jnp.dot(gather[0:128, :], both, preferred_element_type=F32)
    for h in range(2):
        lanes = slice(128 * h, 128 * h + 128)
        codes = both[:, 256 * h : 256 * h + 128] * 256.0 + both[:, 256 * h + 128 : 256 * h + 256]
        x = codes * scale_s[...] + extra[:, lanes] * powers[h, 40:41, :]
        blocks = [x[8 * b : 8 * b + 8] for b in range(16)]
        for i, d in enumerate((1, 2, 4)):
            mult = powers[h, 8 * i : 8 * i + 8, :]
            blocks = [x + mult * pltpu.roll(x, d, 0) for x in blocks]
        lift, whole = powers[h, 24:32, :], powers[h, 32:40, :]
        carry = jnp.zeros((8, 128), F32)
        scan_s[h, 0:8, :] = carry
        for b in range(16):
            total = jnp.broadcast_to(blocks[b][7:8], (8, 128))
            scan_s[h, 8 * b + 1 : 8 * b + 9, :] = blocks[b] + lift * carry
            carry = whole * carry + total
    start = [scan_s[h, 0:128, :] * powers[h, 42:43, :] for h in range(2)]
    upper, lower = split(jnp.concatenate(start, axis=1))
    wide = jnp.concatenate([upper, upper, lower], axis=1)
    rows_s[0:128, 0:128] = extra[:, 256:384] + jnp.dot(
        wide, m1[...], preferred_element_type=F32
    )
    late = [
        start[h] * powers[h, 41:42, :]
        + extra[:, 128 * h : 128 * h + 128] * powers[h, 42:43, :]
        for h in range(2)
    ]
    for b in range(8):
        rows = slice(16 * b, 16 * b + 16)
        power = power_of(
            group_max(jnp.maximum(jnp.abs(late[0][rows]), jnp.abs(late[1][rows])))
        )
        for h in range(2):
            put(h, 16 * b, encode(late[h][rows], power))
        y = rows_s[rows, 0:128]
        power_y = power_of(group_max(jnp.abs(y)))
        y = jnp.where(group == 6, power, jnp.where(group == 7, power_y, encode(y, power_y)))
        put(2, 16 * b, y)
    both = jnp.dot(scatter[...], codes_s[...], preferred_element_type=F32)
    for kind in range(4):
        hi = both[:, 256 * kind : 256 * kind + 128]
        lo = both[:, 256 * kind + 128 : 256 * kind + 256]
        stage[pl.ds(kind, SLOTS, stride=4), :] = hi * 256.0 + lo
    stage_to_send(send_s, 8, 0, code)
    send_all(send_s, recv_s, 2)
    recv_s[me] = send_s[me]

    for b in range(8):
        t0 = b * 8

        def inner(s, acc):
            taps = [row8(filt, t0 + i - s + PAD) for i in range(8)]
            out = []
            for slot in range(2):
                u = u_s[u_row(slot, s), :]
                out += [acc[slot * 8 + i] + taps[i] * u for i in range(8)]
            return tuple(out)

        acc = lax.fori_loop(
            REACH,
            t0 + 8,
            inner,
            tuple(jnp.zeros((8, 128), F32) for _ in range(16)),
            unroll=2,
        )
        for slot in range(2):
            for i in range(8):
                y_s[u_row(slot, t0 + i), :] = acc[slot * 8 + i]

    all_of(send_s, recv_s, 2).wait_recv()
    recv_to_stage(recv_s, 8, 0, uncode)
    for slot in range(2):
        low, high, y_part, q_part = [
            swap_groups(
                [stage[pl.ds(lg * 8 + slot * 4 + kind, 8, stride=64), :] for lg in range(8)]
            )
            for kind in range(4)
        ]
        scale = jnp.exp2(y_part[6]) * (1.0 / FULL)
        scale_y = jnp.exp2(y_part[7]) * (1.0 / FULL)
        scale_q = jnp.exp2(q_part[6]) * (1.0 / FULL)
        for t in range(REACH):
            rows = u_row(slot, t)
            query = z_s[rows, :] + q_part[t] * scale_q
            z_s[rows, :] = query * (y_part[t] * scale_y)

        def last(t, state):
            state = tuple(x * d for x, d in zip(state, decay))
            sums = list(state)
            while len(sums) > 1:
                sums = [x + y for x, y in zip(sums[0::2], sums[1::2])]
            rows = u_row(slot, t)
            z_s[rows, :] = z_s[rows, :] * (y_s[rows, :] + sums[0])
            return state

        lax.fori_loop(
            REACH, STRETCH, last, tuple(x * scale for x in low + high), unroll=2
        )

    @pl.loop(0, 16)
    def _(b):
        rows = pl.ds(pl.multiple_of(b * 8, 8), 8)
        total = jnp.zeros((8, 128), F32)
        for j in range(8):
            z = z_s[pl.ds(b * 64 + j, 8, stride=8), :]
            zn_s[rows, 128 * j : 128 * j + 128] = z
            total = total + z * z
        sq_s[rows, :] = total

    sums = lax.dot_general(
        jnp.ones((8, 128), F32),
        sq_s[...],
        (((1,), (1,)), ((), ())),
        precision=HIGHEST,
        preferred_element_type=F32,
    )
    sq_send[0] = sums
    sq_recv[my_ch] = sums

    @pl.loop(1, n_ch)
    def _(i):
        pltpu.make_async_remote_copy(
            src_ref=sq_send.at[0],
            dst_ref=sq_recv.at[my_ch],
            send_sem=ssem.at[3],
            recv_sem=rsem.at[3],
            device_id={"ch": (my_ch + i) % n_ch},
            device_id_type=MESH,
        ).start()

    every = pltpu.make_async_remote_copy(
        src_ref=sq_recv.at[pl.ds(0, n_ch - 1)],
        dst_ref=sq_recv.at[pl.ds(0, n_ch - 1)],
        send_sem=ssem.at[3],
        recv_sem=rsem.at[3],
        device_id={"ch": (my_ch + 1) % n_ch},
        device_id_type=MESH,
    )
    every.wait_recv()
    total = sq_recv[0]
    for i in range(1, n_ch):
        total = total + sq_recv[i]
    scale = lax.rsqrt(total / float(width_all) + EPS)
    sq_s[...] = jnp.transpose(jnp.broadcast_to(scale[0:1], (128, 128)))

    @pl.loop(0, 8)
    def _(b):
        rows = pl.ds(pl.multiple_of(b * 16, 16), 16)
        by = sq_s[rows, :]
        for j in range(8):
            lanes = slice(128 * j, 128 * j + 128)
            o_ref[rows, lanes] = (zn_s[rows, lanes] * by * gain_ref[:, lanes]).astype(BF16)

    all_of(send_b, recv_b, 0).wait_send()
    all_of(send_e, recv_e, 1).wait_send()
    all_of(send_s, recv_s, 2).wait_send()
    every.wait_send()


def on_device(n_ch, width_all, q_in, k_in, v_in, stretch_of_slot, short_weight, rates, residues, skip, gain):
    vmem = pl.BlockSpec(memory_space=pltpu.VMEM)
    hbm = pl.BlockSpec(memory_space=pltpu.HBM)
    f32 = lambda *shape: pltpu.VMEM(shape, F32)
    bf16 = lambda *shape: pltpu.VMEM(shape, BF16)
    i16 = lambda *shape: pltpu.VMEM(shape, jnp.int16)
    scratch = (
        [bf16(TOKENS, WIDTH)] * 3
        + [pltpu.VMEM((1, SLOTS), jnp.int32), f32(3, TAPS, WIDTH)]
        + [f32(ORDER, WIDTH)] * 2
        + [f32(8, 128), f32(1, WIDTH)]
        + [f32(3, TOKENS * 8, 128)]
        + [f32(TOKENS * 8, 128)] * 3
        + [f32(TOKENS, WIDTH)]
        + [f32(ORDER * 8, 128)] * 2
        + [f32(192, 128), f32((STRETCH + PAD) * 8, 128), f32(512, 128), f32(64, 128), f32(128, 128)]
        + [bf16(256, 128), bf16(128, 128), f32(2, 48, 128)]
        + [bf16(384, 384), bf16(768, 128), f32(128, 384), f32(256, 512), bf16(128, 1024)]
        + [f32(2, 136, 128), f32(128, 128), f32(128, 128)]
        + [bf16(OWNERS, 8, 128)] * 2
        + [i16(OWNERS, 4, 128)] * 2
        + [i16(OWNERS, 8, 128)] * 2
        + [f32(1, 8, 128), f32(n_ch, 8, 128)]
        + [pltpu.SemaphoreType.DMA((4,)), pltpu.SemaphoreType.DMA((4,))]
        + [pltpu.SemaphoreType.DMA((9,))]
    )
    return pl.pallas_call(
        functools.partial(kernel, n_ch, width_all),
        out_shape=pltpu.VMEM((TOKENS, WIDTH), BF16),
        in_specs=[hbm] * 9,
        out_specs=vmem,
        scratch_shapes=scratch,
        compiler_params=pltpu.CompilerParams(collective_id=0, has_side_effects=True),
        name="hyena",
    )(
        q_in,
        k_in,
        v_in,
        stretch_of_slot.reshape(1, SLOTS),
        short_weight,
        rates,
        residues,
        skip.reshape(8, 128),
        gain.reshape(1, WIDTH),
    )


def solution(mesh):
    n_ch = mesh.shape["ch"]

    def body(*args):
        return on_device(n_ch, n_ch * WIDTH, *args)

    in_specs = (
        P("ctx", "ch"),
        P("ctx", "ch"),
        P("ctx", "ch"),
        P(),
        P(None, None, "ch"),
        P(None, "ch"),
        P(None, "ch"),
        P("ch"),
        P("ch"),
    )
    return jax.shard_map(
        body, mesh=mesh, in_specs=in_specs, out_specs=P("ctx", "ch"), check_vma=False
    )
```

```python
import functools

import jax
import jax.numpy as jnp
from jax import lax
from jax.experimental import pallas as pl
from jax.experimental.pallas import tpu as pltpu
from jax.sharding import PartitionSpec as P

F32 = jnp.float32
BF16 = jnp.bfloat16
MESH = pl.DeviceIdType.MESH

TOKENS = 128
WIDTH = 1024
STRETCH = 64
REACH = 6
TAPS = 7
ORDER = 16
OWNERS = 64
GROUP = 16
SLOTS = 128
PAD = 8
EPS = 1e-05
FULL = 32000.0
TINY = 1e-30


def iota(shape, dim):
    return lax.broadcasted_iota(jnp.int32, shape, dim)


def swap_groups(regs):
    regs = list(regs)
    group = iota((8, 128), 1) // GROUP
    for bit in (1, 2, 4):
        low = (group & bit) == 0
        for i in range(8):
            if i & bit:
                continue
            x, y = regs[i], regs[i | bit]
            regs[i] = jnp.where(low, x, pltpu.roll(y, GROUP * bit, 1))
            regs[i | bit] = jnp.where(low, pltpu.roll(x, 128 - GROUP * bit, 1), y)
    return regs


def one_minus_exp_neg(x):
    series = 1.0 - x / 9.0
    for n in (8, 7, 6, 5, 4, 3, 2):
        series = 1.0 - (x / n) * series
    return jnp.where(x < 0.3, x * series, 1.0 - jnp.exp(-x))


def kernel(
    n_ch,
    width_all,
    q_hbm,
    k_hbm,
    v_hbm,
    sos_hbm,
    sw_hbm,
    rates_hbm,
    res_hbm,
    skip_hbm,
    gain_hbm,
    o_ref,
    q_ref,
    k_ref,
    v_ref,
    sos_ref,
    sw_ref,
    rates_ref,
    res_ref,
    skip_ref,
    gain_ref,
    ext,
    u_s,
    y_s,
    z_s,
    zn_s,
    rt,
    am,
    sw,
    filt,
    stage,
    own,
    six,
    gather,
    scatter,
    powers,
    mm,
    m1,
    extra,
    rows_s,
    codes_s,
    scan_s,
    scale_s,
    sq_s,
    send_b,
    recv_b,
    send_e,
    recv_e,
    send_s,
    recv_s,
    sq_send,
    sq_recv,
    ssem,
    rsem,
    isem,
):
    me = lax.axis_index("ctx")
    my_ch = lax.axis_index("ch")
    my_z, my_l = me // 4, me % 4
    my_sub, my_lg = me // 8, me % 8

    barrier = pltpu.get_barrier_semaphore()

    def peer_z(step):
        return (my_z + (2 * (step % 2) - 1) * ((step + 1) // 2) + 16) % 16

    def greet(d):
        pl.semaphore_signal(barrier, 1, device_id={"ctx": d}, device_id_type=MESH)

    @pl.loop(0, 15)
    def _(i):
        for l in range(4):
            greet(peer_z(15 - i) * 4 + l)

    for l in range(1, 4):
        greet(my_z * 4 + (my_l + l) % 4)

    @pl.loop(1, n_ch)
    def _(i):
        pl.semaphore_signal(
            barrier, 1, device_id={"ch": (my_ch + i) % n_ch}, device_id_type=MESH
        )

    def load(i, src, dst):
        copy = pltpu.make_async_copy(src, dst, isem.at[i])
        copy.start()
        return copy

    loads = {
        "rates": load(0, rates_hbm, rates_ref),
        "res": load(1, res_hbm, res_ref),
        "sw": load(2, sw_hbm, sw_ref),
        "k": load(3, k_hbm, k_ref),
        "v": load(4, v_hbm, v_ref),
        "q": load(5, q_hbm, q_ref),
        "sos": load(6, sos_hbm, sos_ref),
        "skip": load(7, skip_hbm, skip_ref),
        "gain": load(8, gain_hbm, gain_ref),
    }

    def send_one(src, dst, sem, d):
        pltpu.make_async_remote_copy(
            src_ref=src.at[d],
            dst_ref=dst.at[me],
            send_sem=ssem.at[sem],
            recv_sem=rsem.at[sem],
            device_id={"ctx": d},
            device_id_type=MESH,
        ).start()

    def send_all(src, dst, sem):
        @pl.loop(0, 15)
        def _(i):
            for l in range(4):
                send_one(src, dst, sem, peer_z(15 - i) * 4 + (my_l + l) % 4)

        for l in range(1, 4):
            send_one(src, dst, sem, my_z * 4 + (my_l + l) % 4)

    def all_of(src, dst, sem):
        return pltpu.make_async_remote_copy(
            src_ref=src.at[pl.ds(0, OWNERS - 1)],
            dst_ref=dst.at[pl.ds(0, OWNERS - 1)],
            send_sem=ssem.at[sem],
            recv_sem=rsem.at[sem],
            device_id={"ctx": (me + 1) % OWNERS},
            device_id_type=MESH,
        )

    def code(x):
        return x.astype(jnp.int32).astype(jnp.int16)

    def uncode(x):
        return x.astype(jnp.int32).astype(F32)

    def narrow(x):
        return x.astype(BF16)

    def widen(x):
        return x.astype(F32)

    def stage_to_send(dst, pitch, first, convert):
        rows = dst.shape[1]

        @pl.loop(0, 8)
        def _(b):
            for i in range(8):
                d = b * 8 + i
                dst[d] = convert(stage[pl.ds(d * pitch + first, rows), :])

    def recv_to_stage(src, pitch, first, convert):
        rows = src.shape[1]

        @pl.loop(0, 8)
        def _(b):
            for i in range(8):
                d = b * 8 + i
                stage[pl.ds(d * pitch + first, rows), :] = convert(src[d])

    def token(array, slot, t):
        return ext[array, pl.ds(pl.multiple_of((slot * STRETCH + t) * 8, 8), 8), :]

    def row8(ref, i):
        return ref[pl.ds(pl.multiple_of(i * 8, 8), 8), :]

    loads["rates"].wait()
    loads["res"].wait()
    loads["sw"].wait()
    for j in range(8):
        lanes = slice(128 * j, 128 * j + 128)
        rate = rates_ref[:, lanes]
        amount = res_ref[:, lanes] * jnp.sqrt(one_minus_exp_neg(2.0 * rate))
        rt[pl.ds(j, ORDER, stride=8), :] = rate
        am[pl.ds(j, ORDER, stride=8), :] = amount
        for a in range(3):
            sw[pl.ds(a * 64 + j, TAPS, stride=8), :] = sw_ref[a, :, lanes]
    for a in range(3):
        sw[a * 64 + 56 : a * 64 + 64, :] = jnp.zeros((8, 128), F32)

    for array, name, ref in ((1, "k", k_ref), (2, "v", v_ref), (0, "q", q_ref)):
        loads[name].wait()
        for slot in range(2):

            @pl.loop(0, 4)
            def _(tb):
                for j in range(8):
                    rows = ref[
                        pl.ds(pl.multiple_of(slot * STRETCH + tb * 16, 16), 16),
                        128 * j : 128 * j + 128,
                    ].astype(F32)
                    start = (slot * STRETCH + tb * 16) * 8 + j
                    ext[array, pl.ds(start, 16, stride=8), :] = rows
    loads["sos"].wait()
    loads["skip"].wait()
    loads["gain"].wait()

    def feature(array, slot, t):
        total = row8(sw, array * 8) * token(array, slot, t)
        for j in range(1, TAPS):
            total = total + row8(sw, array * 8 + j) * token(array, slot, t - j)
        return total

    def u_row(slot, t):
        return pl.ds(pl.multiple_of((slot * STRETCH + t) * 8, 8), 8)

    decay = [jnp.exp(-row8(rt, m)) for m in range(ORDER)]
    end_scale = []
    for slot in range(2):

        def step(t, acc):
            u = feature(1, slot, t) * feature(2, slot, t)
            u_s[u_row(slot, t), :] = u
            return tuple(a * d + u for a, d in zip(acc, decay))

        ends = lax.fori_loop(
            REACH,
            STRETCH,
            step,
            tuple(jnp.zeros((8, 128), F32) for _ in range(ORDER)),
            unroll=2,
        )
        largest = jnp.abs(ends[0])
        for end in ends[1:]:
            largest = jnp.maximum(largest, jnp.abs(end))
        scale = jnp.maximum(largest * 1.0078125, TINY).astype(BF16).astype(F32)
        end_scale.append(scale)
        inverse = FULL / scale
        ends = [jnp.round(end * inverse) for end in ends]
        for h in range(2):
            for lg, reg in enumerate(swap_groups(ends[8 * h : 8 * h + 8])):
                stage[pl.ds(lg * 4 + slot * 2 + h, 8, stride=32), :] = reg
    stage_to_send(send_e, 4, 0, code)

    for slot in range(2):
        q_tail = [token(0, slot, 58 + t) for t in range(6)]
        kinds = (
            [token(1, slot, t) for t in range(6)] + q_tail[4:6],
            [token(2, slot, t) for t in range(6)] + [end_scale[slot]] * 2,
            q_tail[0:2] + [token(1, slot, 58 + t) for t in range(6)],
            q_tail[2:4] + [token(2, slot, 58 + t) for t in range(6)],
        )
        for kind in range(4):
            for lg, reg in enumerate(swap_groups(kinds[kind])):
                stage[pl.ds(lg * 8 + slot * 4 + kind, 8, stride=64), :] = reg
    stage_to_send(send_b, 8, 0, narrow)

    pl.semaphore_wait(barrier, OWNERS - 1 + n_ch - 1)
    send_all(send_b, recv_b, 0)
    send_all(send_e, recv_e, 1)
    recv_b[me] = send_b[me]
    recv_e[me] = send_e[me]

    def ones_where(hit):
        return jnp.where(hit, 1.0, 0.0).astype(BF16)

    sos_row = jnp.broadcast_to(sos_ref[...], (16, SLOTS))
    sublane = iota((16, SLOTS), 0)
    for b in range(16):
        s = sublane + (16 * b - (129 if b >= 8 else 0))
        gather[16 * b : 16 * b + 16, :] = ones_where(sos_row == s)
    sos_column = jnp.transpose(jnp.broadcast_to(sos_ref[...].astype(F32), (SLOTS, SLOTS)))
    scatter[...] = ones_where(sos_column.astype(jnp.int32) == iota((SLOTS, SLOTS), 1))

    filt[0 : PAD * 8, :] = jnp.zeros((PAD * 8, 128), F32)

    def filter_step(d, powers):
        sums = list(powers)
        while len(sums) > 1:
            sums = [x + y for x, y in zip(sums[0::2], sums[1::2])]
        filt[pl.ds(pl.multiple_of((d + PAD) * 8, 8), 8), :] = sums[0]
        return tuple(p * x for p, x in zip(powers, decay))

    lax.fori_loop(
        0, STRETCH, filter_step, tuple(row8(am, m) for m in range(ORDER)), unroll=2
    )
    filt[PAD * 8 : PAD * 8 + 8, :] = filt[PAD * 8 : PAD * 8 + 8, :] + skip_ref[...]

    for slot in range(2):

        for t in range(REACH):
            total = row8(sw, 0) * token(0, slot, t)
            for j in range(1, t + 1):
                total = total + row8(sw, j) * token(0, slot, t - j)
            z_s[u_row(slot, t), :] = total

        @pl.loop(REACH, STRETCH, unroll=2)
        def _(t):
            z_s[u_row(slot, t), :] = feature(0, slot, t)

    def own_modes(table):
        found = []
        for h in range(2):
            for lg, reg in enumerate(swap_groups([row8(table, 8 * h + m) for m in range(8)])):
                own[lg * 8 : lg * 8 + 8, :] = reg
            found.append(own[pl.ds(my_lg * 8 + my_sub, 1), :])
        return found

    own_rates, own_amounts = own_modes(rt), own_modes(am)

    lane128 = iota((8, 128), 1)

    def own_taps(table, first):
        rows = table[pl.ds(first + my_sub, 8, stride=8), :]
        rows = pltpu.roll(rows, (128 - GROUP * my_lg) % 128, 1)
        rows = jnp.where(lane128 < GROUP, rows, 0.0)
        for shift in (16, 32, 64):
            rows = rows + pltpu.roll(rows, shift, 1)
        return rows

    taps_q, taps_k, taps_v = own_taps(sw, 0), own_taps(sw, 64), own_taps(sw, 128)
    own_filter = own_taps(filt, PAD * 8)
    r_row, r_lane = iota((128, 128), 0), iota((128, 128), 1)
    same = (r_row & (GROUP - 1)) == (r_lane & (GROUP - 1))
    g_row, g_lane = r_row >> 4, r_lane >> 4
    inside = same & (g_row < REACH)

    def split(x):
        upper = x.astype(BF16)
        return upper, (x - upper.astype(F32)).astype(BF16)

    def put_mm(part, x):
        lanes = slice(128 * part, 128 * part + 128)
        mm[0:128, lanes], mm[128:256, lanes] = split(x)
        mm[256:384, lanes] = mm[0:128, lanes]

    for h in range(2):
        lift = jnp.exp(-own_rates[h] * (REACH - 1 - g_row).astype(F32))
        put_mm(h, jnp.where(inside, lift, 0.0))
        rate = jnp.transpose(jnp.broadcast_to(own_rates[h], (128, 128)))
        lift = jnp.exp(-rate * (g_lane + 1).astype(F32))
        lift = jnp.where(same & (g_lane < REACH), lift, 0.0)
        upper, lower = split(lift)
        for i, part in enumerate((upper, lower, upper)):
            m1[256 * i + 128 * h : 256 * i + 128 * h + 128, :] = part
    near = jnp.zeros((128, 128), F32)
    inside = inside & (g_lane < REACH)
    for d in range(REACH):
        near = jnp.where(inside & (g_lane - g_row == d), own_filter[d : d + 1], near)
    put_mm(2, near)
    sub8 = iota((8, 128), 0)
    for h in range(2):
        span = own_rates[h] * float(STRETCH)
        for i, d in enumerate((1, 2, 4)):
            powers[h, 8 * i : 8 * i + 8, :] = jnp.where(sub8 >= d, jnp.exp(-span * float(d)), 0.0)
        powers[h, 24:32, :] = jnp.exp(-span * (sub8 + 1).astype(F32))
        powers[h, 32:40, :] = jnp.broadcast_to(jnp.exp(-span * 8.0), (8, 128))
        powers[h, 40:41, :] = jnp.exp(-own_rates[h] * float(STRETCH - REACH))
        powers[h, 41:42, :] = jnp.exp(-own_rates[h] * float(REACH))
        powers[h, 42:43, :] = own_amounts[h]

    def halves(x):
        hi = jnp.floor(x * (1.0 / 256.0))
        return hi, x - 256.0 * hi

    def group_max(x):
        for shift in (16, 32, 64):
            x = jnp.maximum(x, pltpu.roll(x, shift, 1))
        return x

    def power_of(largest):
        return jnp.ceil(jnp.log2(jnp.maximum(largest, TINY)))

    def encode(x, power):
        return jnp.round(x * (jnp.exp2(-power) * FULL))

    def put(kind, rows, x):
        hi, lo = halves(x)
        at = pl.ds(rows, x.shape[0])
        codes_s[at, kind * 256 : kind * 256 + 128] = hi.astype(BF16)
        codes_s[at, kind * 256 + 128 : kind * 256 + 256] = lo.astype(BF16)

    all_of(send_b, recv_b, 0).wait_recv()
    recv_to_stage(recv_b, 8, 0, widen)
    raw = jnp.concatenate(
        [stage[pl.ds(kind, SLOTS, stride=4), :].astype(BF16) for kind in range(4)], axis=1
    )
    rows_s[0:128, 0:256] = jnp.dot(gather[0:128, :], raw[:, 0:256], preferred_element_type=F32)
    rows_s[128:256, :] = jnp.dot(gather[128:256, :], raw, preferred_element_type=F32)
    group = iota((16, 128), 1) >> 4

    @pl.loop(0, 8, unroll=2)
    def _(b):
        first = pl.multiple_of(b * 16, 16)

        def block(kind, before):
            at = pl.ds(pl.multiple_of(before * 128 + b * 16, 16), 16)
            return rows_s[at, kind * 128 : kind * 128 + 128]

        def edge(head, tail, taps):
            total = taps[0:1] * head
            for j in range(1, TAPS):
                mixed = jnp.where(group < 8 - j, head, tail)
                total = total + taps[j : j + 1] * pltpu.roll(mixed, GROUP * j, 1)
            return total

        rows = pl.ds(first, 16)
        head_v, tail_k, tail_v = block(1, 0), block(2, 1), block(3, 1)
        six[rows, :] = edge(block(0, 0), tail_k, taps_k) * edge(head_v, tail_v, taps_v)
        scale = jnp.where(group == 6, head_v * (1.0 / FULL), 0.0)
        for shift in (16, 32, 64):
            scale = scale + pltpu.roll(scale, shift, 1)
        scale_s[rows, :] = scale
        tail_q = jnp.where(group >= 4, pltpu.roll(tail_v, 64, 1), pltpu.roll(tail_k, 32, 1))
        tail_q = jnp.where(group >= 6, block(0, 1), tail_q)
        part = edge(jnp.zeros_like(tail_q), tail_q, taps_q)
        part = jnp.where(group < REACH, part, 0.0)
        power = power_of(group_max(jnp.abs(part)))
        put(3, first, jnp.where(group == 6, power, encode(part, power)))

    upper, lower = split(six[...])
    wide = jnp.concatenate([upper, upper, lower], axis=1)
    extra[...] = jnp.dot(wide, mm[...], preferred_element_type=F32)

    all_of(send_e, recv_e, 1).wait_recv()
    recv_to_stage(recv_e, 4, 0, uncode)
    parts = []
    for h in range(2):
        parts += [x.astype(BF16) for x in halves(stage[pl.ds(h, SLOTS, stride=2), :])]
    both = jnp.concatenate(parts, axis=1)
    both = jnp.dot(gather[0:128, :], both, preferred_element_type=F32)
    for h in range(2):
        lanes = slice(128 * h, 128 * h + 128)
        codes = both[:, 256 * h : 256 * h + 128] * 256.0 + both[:, 256 * h + 128 : 256 * h + 256]
        x = codes * scale_s[...] + extra[:, lanes] * powers[h, 40:41, :]
        blocks = [x[8 * b : 8 * b + 8] for b in range(16)]
        for i, d in enumerate((1, 2, 4)):
            mult = powers[h, 8 * i : 8 * i + 8, :]
            blocks = [x + mult * pltpu.roll(x, d, 0) for x in blocks]
        lift, whole = powers[h, 24:32, :], powers[h, 32:40, :]
        carry = jnp.zeros((8, 128), F32)
        scan_s[h, 0:8, :] = carry
        for b in range(16):
            total = jnp.broadcast_to(blocks[b][7:8], (8, 128))
            scan_s[h, 8 * b + 1 : 8 * b + 9, :] = blocks[b] + lift * carry
            carry = whole * carry + total
    start = [scan_s[h, 0:128, :] * powers[h, 42:43, :] for h in range(2)]
    upper, lower = split(jnp.concatenate(start, axis=1))
    wide = jnp.concatenate([upper, upper, lower], axis=1)
    rows_s[0:128, 0:128] = extra[:, 256:384] + jnp.dot(
        wide, m1[...], preferred_element_type=F32
    )
    late = [
        start[h] * powers[h, 41:42, :]
        + extra[:, 128 * h : 128 * h + 128] * powers[h, 42:43, :]
        for h in range(2)
    ]
    for b in range(8):
        rows = slice(16 * b, 16 * b + 16)
        power = power_of(
            group_max(jnp.maximum(jnp.abs(late[0][rows]), jnp.abs(late[1][rows])))
        )
        for h in range(2):
            put(h, 16 * b, encode(late[h][rows], power))
        y = rows_s[rows, 0:128]
        power_y = power_of(group_max(jnp.abs(y)))
        y = jnp.where(group == 6, power, jnp.where(group == 7, power_y, encode(y, power_y)))
        put(2, 16 * b, y)
    both = jnp.dot(scatter[...], codes_s[...], preferred_element_type=F32)
    for kind in range(4):
        hi = both[:, 256 * kind : 256 * kind + 128]
        lo = both[:, 256 * kind + 128 : 256 * kind + 256]
        stage[pl.ds(kind, SLOTS, stride=4), :] = hi * 256.0 + lo
    stage_to_send(send_s, 8, 0, code)
    send_all(send_s, recv_s, 2)
    recv_s[me] = send_s[me]

    for b in range(8):
        t0 = b * 8

        def inner(s, acc):
            taps = [row8(filt, t0 + i - s + PAD) for i in range(8)]
            out = []
            for slot in range(2):
                u = u_s[u_row(slot, s), :]
                out += [acc[slot * 8 + i] + taps[i] * u for i in range(8)]
            return tuple(out)

        acc = lax.fori_loop(
            REACH,
            t0 + 8,
            inner,
            tuple(jnp.zeros((8, 128), F32) for _ in range(16)),
            unroll=2,
        )
        for slot in range(2):
            for i in range(8):
                y_s[u_row(slot, t0 + i), :] = acc[slot * 8 + i]

    all_of(send_s, recv_s, 2).wait_recv()
    recv_to_stage(recv_s, 8, 0, uncode)
    for slot in range(2):
        low, high, y_part, q_part = [
            swap_groups(
                [stage[pl.ds(lg * 8 + slot * 4 + kind, 8, stride=64), :] for lg in range(8)]
            )
            for kind in range(4)
        ]
        scale = jnp.exp2(y_part[6]) * (1.0 / FULL)
        scale_y = jnp.exp2(y_part[7]) * (1.0 / FULL)
        scale_q = jnp.exp2(q_part[6]) * (1.0 / FULL)
        for t in range(REACH):
            rows = u_row(slot, t)
            query = z_s[rows, :] + q_part[t] * scale_q
            z_s[rows, :] = query * (y_part[t] * scale_y)

        def last(t, state):
            state = tuple(x * d for x, d in zip(state, decay))
            sums = list(state)
            while len(sums) > 1:
                sums = [x + y for x, y in zip(sums[0::2], sums[1::2])]
            rows = u_row(slot, t)
            z_s[rows, :] = z_s[rows, :] * (y_s[rows, :] + sums[0])
            return state

        state = lax.fori_loop(
            REACH, STRETCH - 2, last, tuple(x * scale for x in low + high), unroll=4
        )
        for t in (STRETCH - 2, STRETCH - 1):
            state = last(t, state)

    @pl.loop(0, 16)
    def _(b):
        rows = pl.ds(pl.multiple_of(b * 8, 8), 8)
        total = jnp.zeros((8, 128), F32)
        for j in range(8):
            z = z_s[pl.ds(b * 64 + j, 8, stride=8), :]
            lanes = slice(128 * j, 128 * j + 128)
            zn_s[rows, lanes] = z * gain_ref[:, lanes]
            total = total + z * z
        sq_s[rows, :] = total

    sums = lax.dot_general(
        jnp.ones((8, 256), BF16),
        jnp.concatenate(split(sq_s[...]), axis=1),
        (((1,), (1,)), ((), ())),
        preferred_element_type=F32,
    )
    sq_send[0] = sums[0:1]
    sq_recv[my_ch] = sums[0:1]

    @pl.loop(1, n_ch)
    def _(i):
        pltpu.make_async_remote_copy(
            src_ref=sq_send.at[0],
            dst_ref=sq_recv.at[my_ch],
            send_sem=ssem.at[3],
            recv_sem=rsem.at[3],
            device_id={"ch": (my_ch + i) % n_ch},
            device_id_type=MESH,
        ).start()

    every = pltpu.make_async_remote_copy(
        src_ref=sq_recv.at[pl.ds(0, n_ch - 1)],
        dst_ref=sq_recv.at[pl.ds(0, n_ch - 1)],
        send_sem=ssem.at[3],
        recv_sem=rsem.at[3],
        device_id={"ch": (my_ch + 1) % n_ch},
        device_id_type=MESH,
    )
    every.wait_recv()
    total = sq_recv[0]
    for i in range(1, n_ch):
        total = total + sq_recv[i]
    scale = lax.rsqrt(total / float(width_all) + EPS)
    sq_s[...] = jnp.transpose(jnp.broadcast_to(scale, (128, 128)))

    @pl.loop(0, 8)
    def _(b):
        rows = pl.ds(pl.multiple_of(b * 16, 16), 16)
        by = sq_s[rows, :]
        for j in range(8):
            lanes = slice(128 * j, 128 * j + 128)
            o_ref[rows, lanes] = (zn_s[rows, lanes] * by).astype(BF16)

    all_of(send_b, recv_b, 0).wait_send()
    all_of(send_e, recv_e, 1).wait_send()
    all_of(send_s, recv_s, 2).wait_send()
    every.wait_send()


def on_device(n_ch, width_all, q_in, k_in, v_in, stretch_of_slot, short_weight, rates, residues, skip, gain):
    vmem = pl.BlockSpec(memory_space=pltpu.VMEM)
    hbm = pl.BlockSpec(memory_space=pltpu.HBM)
    f32 = lambda *shape: pltpu.VMEM(shape, F32)
    bf16 = lambda *shape: pltpu.VMEM(shape, BF16)
    i16 = lambda *shape: pltpu.VMEM(shape, jnp.int16)
    scratch = (
        [bf16(TOKENS, WIDTH)] * 3
        + [pltpu.VMEM((1, SLOTS), jnp.int32), f32(3, TAPS, WIDTH)]
        + [f32(ORDER, WIDTH)] * 2
        + [f32(8, 128), f32(1, WIDTH)]
        + [f32(3, TOKENS * 8, 128)]
        + [f32(TOKENS * 8, 128)] * 3
        + [f32(TOKENS, WIDTH)]
        + [f32(ORDER * 8, 128)] * 2
        + [f32(192, 128), f32((STRETCH + PAD) * 8, 128), f32(512, 128), f32(64, 128), f32(128, 128)]
        + [bf16(256, 128), bf16(128, 128), f32(2, 48, 128)]
        + [bf16(384, 384), bf16(768, 128), f32(128, 384), f32(256, 512), bf16(128, 1024)]
        + [f32(2, 136, 128), f32(128, 128), f32(128, 128)]
        + [bf16(OWNERS, 8, 128)] * 2
        + [i16(OWNERS, 4, 128)] * 2
        + [i16(OWNERS, 8, 128)] * 2
        + [f32(1, 1, 128), f32(n_ch, 1, 128)]
        + [pltpu.SemaphoreType.DMA((4,)), pltpu.SemaphoreType.DMA((4,))]
        + [pltpu.SemaphoreType.DMA((9,))]
    )
    return pl.pallas_call(
        functools.partial(kernel, n_ch, width_all),
        out_shape=pltpu.VMEM((TOKENS, WIDTH), BF16),
        in_specs=[hbm] * 9,
        out_specs=vmem,
        scratch_shapes=scratch,
        compiler_params=pltpu.CompilerParams(collective_id=0, has_side_effects=True),
        name="hyena",
    )(
        q_in,
        k_in,
        v_in,
        stretch_of_slot.reshape(1, SLOTS),
        short_weight,
        rates,
        residues,
        skip.reshape(8, 128),
        gain.reshape(1, WIDTH),
    )


def solution(mesh):
    n_ch = mesh.shape["ch"]

    def body(*args):
        return on_device(n_ch, n_ch * WIDTH, *args)

    in_specs = (
        P("ctx", "ch"),
        P("ctx", "ch"),
        P("ctx", "ch"),
        P(),
        P(None, None, "ch"),
        P(None, "ch"),
        P(None, "ch"),
        P("ch"),
        P("ch"),
    )
    return jax.shard_map(
        body, mesh=mesh, in_specs=in_specs, out_specs=P("ctx", "ch"), check_vma=False
    )
```

```python
import functools

import jax
import jax.numpy as jnp
from jax import lax
from jax.experimental import pallas as pl
from jax.experimental.pallas import tpu as pltpu
from jax.sharding import PartitionSpec as P

F32 = jnp.float32
BF16 = jnp.bfloat16
MESH = pl.DeviceIdType.MESH

TOKENS = 128
WIDTH = 1024
STRETCH = 64
REACH = 6
TAPS = 7
ORDER = 16
OWNERS = 64
GROUP = 16
SLOTS = 128
PAD = 8
EPS = 1e-05
FULL = 32000.0
TINY = 1e-30


def iota(shape, dim):
    return lax.broadcasted_iota(jnp.int32, shape, dim)


def swap_groups(regs):
    regs = list(regs)
    group = iota((8, 128), 1) // GROUP
    for bit in (1, 2, 4):
        low = (group & bit) == 0
        for i in range(8):
            if i & bit:
                continue
            x, y = regs[i], regs[i | bit]
            regs[i] = jnp.where(low, x, pltpu.roll(y, GROUP * bit, 1))
            regs[i | bit] = jnp.where(low, pltpu.roll(x, 128 - GROUP * bit, 1), y)
    return regs


def one_minus_exp_neg(x):
    series = 1.0 - x / 9.0
    for n in (8, 7, 6, 5, 4, 3, 2):
        series = 1.0 - (x / n) * series
    return jnp.where(x < 0.3, x * series, 1.0 - jnp.exp(-x))


def kernel(
    n_ch,
    width_all,
    q_hbm,
    k_hbm,
    v_hbm,
    sos_hbm,
    sw_hbm,
    rates_hbm,
    res_hbm,
    skip_hbm,
    gain_hbm,
    o_ref,
    q_ref,
    k_ref,
    v_ref,
    sos_ref,
    sw_ref,
    rates_ref,
    res_ref,
    skip_ref,
    gain_ref,
    ext,
    u_s,
    y_s,
    z_s,
    zn_s,
    rt,
    am,
    sw,
    filt,
    stage,
    stage_e,
    own,
    six,
    gather,
    scatter,
    powers,
    mm,
    m1,
    extra,
    rows_s,
    codes_s,
    scan_s,
    scale_s,
    sq_s,
    send_b,
    recv_b,
    send_e,
    recv_e,
    send_s,
    recv_s,
    sq_send,
    sq_recv,
    ssem,
    rsem,
    isem,
):
    me = lax.axis_index("ctx")
    my_ch = lax.axis_index("ch")
    my_z, my_l = me // 4, me % 4
    my_sub, my_lg = me // 8, me % 8

    barrier = pltpu.get_barrier_semaphore()

    def peer_z(step):
        return (my_z + (2 * (step % 2) - 1) * ((step + 1) // 2) + 16) % 16

    def greet(d):
        pl.semaphore_signal(barrier, 1, device_id={"ctx": d}, device_id_type=MESH)

    @pl.loop(0, 15)
    def _(i):
        for l in range(4):
            greet(peer_z(15 - i) * 4 + l)

    for l in range(1, 4):
        greet(my_z * 4 + (my_l + l) % 4)

    @pl.loop(1, n_ch)
    def _(i):
        pl.semaphore_signal(
            barrier, 1, device_id={"ch": (my_ch + i) % n_ch}, device_id_type=MESH
        )

    def load(i, src, dst):
        copy = pltpu.make_async_copy(src, dst, isem.at[i])
        copy.start()
        return copy

    loads = {
        "rates": load(0, rates_hbm, rates_ref),
        "res": load(1, res_hbm, res_ref),
        "sw": load(2, sw_hbm, sw_ref),
        "k": load(3, k_hbm, k_ref),
        "v": load(4, v_hbm, v_ref),
        "q": load(5, q_hbm, q_ref),
        "sos": load(6, sos_hbm, sos_ref),
        "skip": load(7, skip_hbm, skip_ref),
        "gain": load(8, gain_hbm, gain_ref),
    }

    def send_one(src, dst, sem, d):
        pltpu.make_async_remote_copy(
            src_ref=src.at[d],
            dst_ref=dst.at[me],
            send_sem=ssem.at[sem],
            recv_sem=rsem.at[sem],
            device_id={"ctx": d},
            device_id_type=MESH,
        ).start()

    def send_all(*sets):
        @pl.loop(0, 15)
        def _(i):
            for l in range(4):
                for one in sets:
                    send_one(*one, peer_z(15 - i) * 4 + (my_l + l) % 4)

        for l in range(1, 4):
            for one in sets:
                send_one(*one, my_z * 4 + (my_l + l) % 4)

    def all_of(src, dst, sem):
        return pltpu.make_async_remote_copy(
            src_ref=src.at[pl.ds(0, OWNERS - 1)],
            dst_ref=dst.at[pl.ds(0, OWNERS - 1)],
            send_sem=ssem.at[sem],
            recv_sem=rsem.at[sem],
            device_id={"ctx": (me + 1) % OWNERS},
            device_id_type=MESH,
        )

    def code(x):
        return x.astype(jnp.int32).astype(jnp.int16)

    def uncode(x):
        return x.astype(jnp.int32).astype(F32)

    def narrow(x):
        return x.astype(BF16)

    def widen(x):
        return x.astype(F32)

    def stage_to_send(dst, pitch, first, convert, stage=stage):
        rows = dst.shape[1]

        @pl.loop(0, 8)
        def _(b):
            for i in range(8):
                d = b * 8 + i
                dst[d] = convert(stage[pl.ds(d * pitch + first, rows), :])

    def recv_to_stage(src, pitch, first, convert, stage=stage):
        rows = src.shape[1]

        @pl.loop(0, 8)
        def _(b):
            for i in range(8):
                d = b * 8 + i
                stage[pl.ds(d * pitch + first, rows), :] = convert(src[d])

    def token(array, slot, t):
        return ext[array, pl.ds(pl.multiple_of((slot * STRETCH + t) * 8, 8), 8), :]

    def row8(ref, i):
        return ref[pl.ds(pl.multiple_of(i * 8, 8), 8), :]

    loads["rates"].wait()
    loads["res"].wait()
    loads["sw"].wait()
    for j in range(8):
        lanes = slice(128 * j, 128 * j + 128)
        rate = rates_ref[:, lanes]
        amount = res_ref[:, lanes] * jnp.sqrt(one_minus_exp_neg(2.0 * rate))
        rt[pl.ds(j, ORDER, stride=8), :] = rate
        am[pl.ds(j, ORDER, stride=8), :] = amount
        for a in range(3):
            sw[pl.ds(a * 64 + j, TAPS, stride=8), :] = sw_ref[a, :, lanes]
    for a in range(3):
        sw[a * 64 + 56 : a * 64 + 64, :] = jnp.zeros((8, 128), F32)

    for array, name, ref in ((1, "k", k_ref), (2, "v", v_ref), (0, "q", q_ref)):
        loads[name].wait()
        for slot in range(2):

            @pl.loop(0, 4)
            def _(tb):
                for j in range(8):
                    rows = ref[
                        pl.ds(pl.multiple_of(slot * STRETCH + tb * 16, 16), 16),
                        128 * j : 128 * j + 128,
                    ].astype(F32)
                    start = (slot * STRETCH + tb * 16) * 8 + j
                    ext[array, pl.ds(start, 16, stride=8), :] = rows
    loads["sos"].wait()
    loads["skip"].wait()
    loads["gain"].wait()

    def feature(array, slot, t):
        total = row8(sw, array * 8) * token(array, slot, t)
        for j in range(1, TAPS):
            total = total + row8(sw, array * 8 + j) * token(array, slot, t - j)
        return total

    def u_row(slot, t):
        return pl.ds(pl.multiple_of((slot * STRETCH + t) * 8, 8), 8)

    decay = [jnp.exp(-row8(rt, m)) for m in range(ORDER)]
    end_scale = []
    for slot in range(2):

        def step(t, acc):
            u = feature(1, slot, t) * feature(2, slot, t)
            u_s[u_row(slot, t), :] = u
            return tuple(a * d + u for a, d in zip(acc, decay))

        ends = lax.fori_loop(
            REACH,
            STRETCH,
            step,
            tuple(jnp.zeros((8, 128), F32) for _ in range(ORDER)),
            unroll=2,
        )
        largest = jnp.abs(ends[0])
        for end in ends[1:]:
            largest = jnp.maximum(largest, jnp.abs(end))
        scale = jnp.maximum(largest * 1.0078125, TINY).astype(BF16).astype(F32)
        end_scale.append(scale)
        inverse = FULL / scale
        ends = [jnp.round(end * inverse) for end in ends]
        for h in range(2):
            for lg, reg in enumerate(swap_groups(ends[8 * h : 8 * h + 8])):
                stage[pl.ds(lg * 4 + slot * 2 + h, 8, stride=32), :] = reg
    stage_to_send(send_e, 4, 0, code)

    for slot in range(2):
        q_tail = [token(0, slot, 58 + t) for t in range(6)]
        kinds = (
            [token(1, slot, t) for t in range(6)] + q_tail[4:6],
            [token(2, slot, t) for t in range(6)] + [end_scale[slot]] * 2,
            q_tail[0:2] + [token(1, slot, 58 + t) for t in range(6)],
            q_tail[2:4] + [token(2, slot, 58 + t) for t in range(6)],
        )
        for kind in range(4):
            for lg, reg in enumerate(swap_groups(kinds[kind])):
                stage[pl.ds(lg * 8 + slot * 4 + kind, 8, stride=64), :] = reg
    stage_to_send(send_b, 8, 0, narrow)

    pl.semaphore_wait(barrier, OWNERS - 1 + n_ch - 1)
    send_all((send_b, recv_b, 0), (send_e, recv_e, 1))
    recv_b[me] = send_b[me]
    recv_e[me] = send_e[me]

    def ones_where(hit):
        return jnp.where(hit, 1.0, 0.0).astype(BF16)

    sos_row = jnp.broadcast_to(sos_ref[...], (16, SLOTS))
    sublane = iota((16, SLOTS), 0)
    for b in range(16):
        s = sublane + (16 * b - (129 if b >= 8 else 0))
        gather[16 * b : 16 * b + 16, :] = ones_where(sos_row == s)
    sos_column = jnp.transpose(jnp.broadcast_to(sos_ref[...].astype(F32), (SLOTS, SLOTS)))
    scatter[...] = ones_where(sos_column.astype(jnp.int32) == iota((SLOTS, SLOTS), 1))

    filt[0 : PAD * 8, :] = jnp.zeros((PAD * 8, 128), F32)

    def filter_step(d, powers):
        sums = list(powers)
        while len(sums) > 1:
            sums = [x + y for x, y in zip(sums[0::2], sums[1::2])]
        filt[pl.ds(pl.multiple_of((d + PAD) * 8, 8), 8), :] = sums[0]
        return tuple(p * x for p, x in zip(powers, decay))

    lax.fori_loop(
        0, STRETCH, filter_step, tuple(row8(am, m) for m in range(ORDER)), unroll=2
    )
    filt[PAD * 8 : PAD * 8 + 8, :] = filt[PAD * 8 : PAD * 8 + 8, :] + skip_ref[...]

    for slot in range(2):

        for t in range(REACH):
            total = row8(sw, 0) * token(0, slot, t)
            for j in range(1, t + 1):
                total = total + row8(sw, j) * token(0, slot, t - j)
            z_s[u_row(slot, t), :] = total

        @pl.loop(REACH, STRETCH, unroll=2)
        def _(t):
            z_s[u_row(slot, t), :] = feature(0, slot, t)

    def own_modes(table):
        found = []
        for h in range(2):
            for lg, reg in enumerate(swap_groups([row8(table, 8 * h + m) for m in range(8)])):
                own[lg * 8 : lg * 8 + 8, :] = reg
            found.append(own[pl.ds(my_lg * 8 + my_sub, 1), :])
        return found

    own_rates, own_amounts = own_modes(rt), own_modes(am)

    lane128 = iota((8, 128), 1)

    def own_taps(table, first):
        rows = table[pl.ds(first + my_sub, 8, stride=8), :]
        rows = pltpu.roll(rows, (128 - GROUP * my_lg) % 128, 1)
        rows = jnp.where(lane128 < GROUP, rows, 0.0)
        for shift in (16, 32, 64):
            rows = rows + pltpu.roll(rows, shift, 1)
        return rows

    taps_q, taps_k, taps_v = own_taps(sw, 0), own_taps(sw, 64), own_taps(sw, 128)
    own_filter = own_taps(filt, PAD * 8)
    r_row, r_lane = iota((128, 128), 0), iota((128, 128), 1)
    same = (r_row & (GROUP - 1)) == (r_lane & (GROUP - 1))
    g_row, g_lane = r_row >> 4, r_lane >> 4
    inside = same & (g_row < REACH)

    def split(x):
        upper = x.astype(BF16)
        return upper, (x - upper.astype(F32)).astype(BF16)

    def put_mm(part, x):
        lanes = slice(128 * part, 128 * part + 128)
        mm[0:128, lanes], mm[128:256, lanes] = split(x)
        mm[256:384, lanes] = mm[0:128, lanes]

    for h in range(2):
        lift = jnp.exp(-own_rates[h] * (REACH - 1 - g_row).astype(F32))
        put_mm(h, jnp.where(inside, lift, 0.0))
        rate = jnp.transpose(jnp.broadcast_to(own_rates[h], (128, 128)))
        lift = jnp.exp(-rate * (g_lane + 1).astype(F32))
        lift = jnp.where(same & (g_lane < REACH), lift, 0.0)
        upper, lower = split(lift)
        for i, part in enumerate((upper, lower, upper)):
            m1[256 * i + 128 * h : 256 * i + 128 * h + 128, :] = part
    near = jnp.zeros((128, 128), F32)
    inside = inside & (g_lane < REACH)
    for d in range(REACH):
        near = jnp.where(inside & (g_lane - g_row == d), own_filter[d : d + 1], near)
    put_mm(2, near)
    sub8 = iota((8, 128), 0)
    for h in range(2):
        span = own_rates[h] * float(STRETCH)
        for i, d in enumerate((1, 2, 4)):
            powers[h, 8 * i : 8 * i + 8, :] = jnp.where(sub8 >= d, jnp.exp(-span * float(d)), 0.0)
        powers[h, 24:32, :] = jnp.exp(-span * (sub8 + 1).astype(F32))
        powers[h, 32:40, :] = jnp.broadcast_to(jnp.exp(-span * 8.0), (8, 128))
        powers[h, 40:41, :] = jnp.exp(-own_rates[h] * float(STRETCH - REACH))
        powers[h, 41:42, :] = jnp.exp(-own_rates[h] * float(REACH))
        powers[h, 42:43, :] = own_amounts[h]

    def halves(x):
        hi = jnp.floor(x * (1.0 / 256.0))
        return hi, x - 256.0 * hi

    def group_max(x):
        for shift in (16, 32, 64):
            x = jnp.maximum(x, pltpu.roll(x, shift, 1))
        return x

    def power_of(largest):
        return jnp.ceil(jnp.log2(jnp.maximum(largest, TINY)))

    def encode(x, power):
        return jnp.round(x * (jnp.exp2(-power) * FULL))

    def put(kind, rows, x):
        hi, lo = halves(x)
        at = pl.ds(rows, x.shape[0])
        codes_s[at, kind * 256 : kind * 256 + 128] = hi.astype(BF16)
        codes_s[at, kind * 256 + 128 : kind * 256 + 256] = lo.astype(BF16)

    all_of(send_b, recv_b, 0).wait_recv()
    recv_to_stage(recv_b, 8, 0, widen)
    all_of(send_e, recv_e, 1).wait_recv()
    recv_to_stage(recv_e, 4, 0, uncode, stage_e)
    raw = jnp.concatenate(
        [stage[pl.ds(kind, SLOTS, stride=4), :].astype(BF16) for kind in range(4)], axis=1
    )
    rows_s[0:128, 0:256] = jnp.dot(gather[0:128, :], raw[:, 0:256], preferred_element_type=F32)
    rows_s[128:256, :] = jnp.dot(gather[128:256, :], raw, preferred_element_type=F32)
    group = iota((16, 128), 1) >> 4

    for b in range(8):
        first = b * 16

        def block(kind, before):
            at = pl.ds(before * 128 + b * 16, 16)
            return rows_s[at, kind * 128 : kind * 128 + 128]

        def edge(head, tail, taps):
            total = taps[0:1] * head
            for j in range(1, TAPS):
                mixed = jnp.where(group < 8 - j, head, tail)
                total = total + taps[j : j + 1] * pltpu.roll(mixed, GROUP * j, 1)
            return total

        rows = pl.ds(first, 16)
        head_v, tail_k, tail_v = block(1, 0), block(2, 1), block(3, 1)
        six[rows, :] = edge(block(0, 0), tail_k, taps_k) * edge(head_v, tail_v, taps_v)
        scale = jnp.where(group == 6, head_v * (1.0 / FULL), 0.0)
        for shift in (16, 32, 64):
            scale = scale + pltpu.roll(scale, shift, 1)
        scale_s[rows, :] = scale
        tail_q = jnp.where(group >= 4, pltpu.roll(tail_v, 64, 1), pltpu.roll(tail_k, 32, 1))
        tail_q = jnp.where(group >= 6, block(0, 1), tail_q)
        part = edge(jnp.zeros_like(tail_q), tail_q, taps_q)
        part = jnp.where(group < REACH, part, 0.0)
        power = power_of(group_max(jnp.abs(part)))
        put(3, first, jnp.where(group == 6, power, encode(part, power)))

    upper, lower = split(six[...])
    wide = jnp.concatenate([upper, upper, lower], axis=1)
    extra[...] = jnp.dot(wide, mm[...], preferred_element_type=F32)

    parts = []
    for h in range(2):
        parts += [x.astype(BF16) for x in halves(stage_e[pl.ds(h, SLOTS, stride=2), :])]
    both = jnp.concatenate(parts, axis=1)
    both = jnp.dot(gather[0:128, :], both, preferred_element_type=F32)
    for h in range(2):
        lanes = slice(128 * h, 128 * h + 128)
        codes = both[:, 256 * h : 256 * h + 128] * 256.0 + both[:, 256 * h + 128 : 256 * h + 256]
        x = codes * scale_s[...] + extra[:, lanes] * powers[h, 40:41, :]
        blocks = [x[8 * b : 8 * b + 8] for b in range(16)]
        for i, d in enumerate((1, 2, 4)):
            mult = powers[h, 8 * i : 8 * i + 8, :]
            blocks = [x + mult * pltpu.roll(x, d, 0) for x in blocks]
        lift, whole = powers[h, 24:32, :], powers[h, 32:40, :]
        carry = jnp.zeros((8, 128), F32)
        scan_s[h, 0:8, :] = carry
        for b in range(16):
            total = jnp.broadcast_to(blocks[b][7:8], (8, 128))
            scan_s[h, 8 * b + 1 : 8 * b + 9, :] = blocks[b] + lift * carry
            carry = whole * carry + total
    start = [scan_s[h, 0:128, :] * powers[h, 42:43, :] for h in range(2)]
    upper, lower = split(jnp.concatenate(start, axis=1))
    wide = jnp.concatenate([upper, upper, lower], axis=1)
    rows_s[0:128, 0:128] = extra[:, 256:384] + jnp.dot(
        wide, m1[...], preferred_element_type=F32
    )
    late = [
        start[h] * powers[h, 41:42, :]
        + extra[:, 128 * h : 128 * h + 128] * powers[h, 42:43, :]
        for h in range(2)
    ]
    for b in range(8):
        rows = slice(16 * b, 16 * b + 16)
        power = power_of(
            group_max(jnp.maximum(jnp.abs(late[0][rows]), jnp.abs(late[1][rows])))
        )
        for h in range(2):
            put(h, 16 * b, encode(late[h][rows], power))
        y = rows_s[rows, 0:128]
        power_y = power_of(group_max(jnp.abs(y)))
        y = jnp.where(group == 6, power, jnp.where(group == 7, power_y, encode(y, power_y)))
        put(2, 16 * b, y)
    both = jnp.dot(scatter[...], codes_s[...], preferred_element_type=F32)
    for kind in range(4):
        hi = both[:, 256 * kind : 256 * kind + 128]
        lo = both[:, 256 * kind + 128 : 256 * kind + 256]
        stage[pl.ds(kind, SLOTS, stride=4), :] = hi * 256.0 + lo
    stage_to_send(send_s, 8, 0, code)
    send_all((send_s, recv_s, 2))
    recv_s[me] = send_s[me]

    for b in range(8):
        t0 = b * 8

        def inner(s, acc):
            taps = [row8(filt, t0 + i - s + PAD) for i in range(8)]
            out = []
            for slot in range(2):
                u = u_s[u_row(slot, s), :]
                out += [acc[slot * 8 + i] + taps[i] * u for i in range(8)]
            return tuple(out)

        acc = lax.fori_loop(
            REACH,
            t0 + 8,
            inner,
            tuple(jnp.zeros((8, 128), F32) for _ in range(16)),
            unroll=2,
        )
        for slot in range(2):
            for i in range(8):
                y_s[u_row(slot, t0 + i), :] = acc[slot * 8 + i]

    all_of(send_s, recv_s, 2).wait_recv()
    recv_to_stage(recv_s, 8, 0, uncode)
    for slot in range(2):
        low, high, y_part, q_part = [
            swap_groups(
                [stage[pl.ds(lg * 8 + slot * 4 + kind, 8, stride=64), :] for lg in range(8)]
            )
            for kind in range(4)
        ]
        scale = jnp.exp2(y_part[6]) * (1.0 / FULL)
        scale_y = jnp.exp2(y_part[7]) * (1.0 / FULL)
        scale_q = jnp.exp2(q_part[6]) * (1.0 / FULL)
        for t in range(REACH):
            rows = u_row(slot, t)
            query = z_s[rows, :] + q_part[t] * scale_q
            z_s[rows, :] = query * (y_part[t] * scale_y)

        def last(t, state):
            state = tuple(x * d for x, d in zip(state, decay))
            sums = list(state)
            while len(sums) > 1:
                sums = [x + y for x, y in zip(sums[0::2], sums[1::2])]
            rows = u_row(slot, t)
            z_s[rows, :] = z_s[rows, :] * (y_s[rows, :] + sums[0])
            return state

        state = lax.fori_loop(
            REACH, STRETCH - 2, last, tuple(x * scale for x in low + high), unroll=4
        )
        for t in (STRETCH - 2, STRETCH - 1):
            state = last(t, state)

    @pl.loop(0, 16)
    def _(b):
        rows = pl.ds(pl.multiple_of(b * 8, 8), 8)
        total = jnp.zeros((8, 128), F32)
        for j in range(8):
            z = z_s[pl.ds(b * 64 + j, 8, stride=8), :]
            lanes = slice(128 * j, 128 * j + 128)
            zn_s[rows, lanes] = z * gain_ref[:, lanes]
            total = total + z * z
        sq_s[rows, :] = total

    sums = lax.dot_general(
        jnp.ones((8, 256), BF16),
        jnp.concatenate(split(sq_s[...]), axis=1),
        (((1,), (1,)), ((), ())),
        preferred_element_type=F32,
    )
    sq_send[0] = sums[0:1]
    sq_recv[my_ch] = sums[0:1]

    @pl.loop(1, n_ch)
    def _(i):
        pltpu.make_async_remote_copy(
            src_ref=sq_send.at[0],
            dst_ref=sq_recv.at[my_ch],
            send_sem=ssem.at[3],
            recv_sem=rsem.at[3],
            device_id={"ch": (my_ch + i) % n_ch},
            device_id_type=MESH,
        ).start()

    every = pltpu.make_async_remote_copy(
        src_ref=sq_recv.at[pl.ds(0, n_ch - 1)],
        dst_ref=sq_recv.at[pl.ds(0, n_ch - 1)],
        send_sem=ssem.at[3],
        recv_sem=rsem.at[3],
        device_id={"ch": (my_ch + 1) % n_ch},
        device_id_type=MESH,
    )
    every.wait_recv()
    total = sq_recv[0]
    for i in range(1, n_ch):
        total = total + sq_recv[i]
    scale = lax.rsqrt(total / float(width_all) + EPS)
    sq_s[...] = jnp.transpose(jnp.broadcast_to(scale, (128, 128)))

    @pl.loop(0, 8)
    def _(b):
        rows = pl.ds(pl.multiple_of(b * 16, 16), 16)
        by = sq_s[rows, :]
        for j in range(8):
            lanes = slice(128 * j, 128 * j + 128)
            o_ref[rows, lanes] = (zn_s[rows, lanes] * by).astype(BF16)

    all_of(send_b, recv_b, 0).wait_send()
    all_of(send_e, recv_e, 1).wait_send()
    all_of(send_s, recv_s, 2).wait_send()
    every.wait_send()


def on_device(n_ch, width_all, q_in, k_in, v_in, stretch_of_slot, short_weight, rates, residues, skip, gain):
    vmem = pl.BlockSpec(memory_space=pltpu.VMEM)
    hbm = pl.BlockSpec(memory_space=pltpu.HBM)
    f32 = lambda *shape: pltpu.VMEM(shape, F32)
    bf16 = lambda *shape: pltpu.VMEM(shape, BF16)
    i16 = lambda *shape: pltpu.VMEM(shape, jnp.int16)
    scratch = (
        [bf16(TOKENS, WIDTH)] * 3
        + [pltpu.VMEM((1, SLOTS), jnp.int32), f32(3, TAPS, WIDTH)]
        + [f32(ORDER, WIDTH)] * 2
        + [f32(8, 128), f32(1, WIDTH)]
        + [f32(3, TOKENS * 8, 128)]
        + [f32(TOKENS * 8, 128)] * 3
        + [f32(TOKENS, WIDTH)]
        + [f32(ORDER * 8, 128)] * 2
        + [f32(192, 128), f32((STRETCH + PAD) * 8, 128), f32(512, 128), f32(256, 128), f32(64, 128), f32(128, 128)]
        + [bf16(256, 128), bf16(128, 128), f32(2, 48, 128)]
        + [bf16(384, 384), bf16(768, 128), f32(128, 384), f32(256, 512), bf16(128, 1024)]
        + [f32(2, 136, 128), f32(128, 128), f32(128, 128)]
        + [bf16(OWNERS, 8, 128)] * 2
        + [i16(OWNERS, 4, 128)] * 2
        + [i16(OWNERS, 8, 128)] * 2
        + [f32(1, 1, 128), f32(n_ch, 1, 128)]
        + [pltpu.SemaphoreType.DMA((4,)), pltpu.SemaphoreType.DMA((4,))]
        + [pltpu.SemaphoreType.DMA((9,))]
    )
    return pl.pallas_call(
        functools.partial(kernel, n_ch, width_all),
        out_shape=pltpu.VMEM((TOKENS, WIDTH), BF16),
        in_specs=[hbm] * 9,
        out_specs=vmem,
        scratch_shapes=scratch,
        compiler_params=pltpu.CompilerParams(collective_id=0, has_side_effects=True),
        name="hyena",
    )(
        q_in,
        k_in,
        v_in,
        stretch_of_slot.reshape(1, SLOTS),
        short_weight,
        rates,
        residues,
        skip.reshape(8, 128),
        gain.reshape(1, WIDTH),
    )


def solution(mesh):
    n_ch = mesh.shape["ch"]

    def body(*args):
        return on_device(n_ch, n_ch * WIDTH, *args)

    in_specs = (
        P("ctx", "ch"),
        P("ctx", "ch"),
        P("ctx", "ch"),
        P(),
        P(None, None, "ch"),
        P(None, "ch"),
        P(None, "ch"),
        P("ch"),
        P("ch"),
    )
    return jax.shard_map(
        body, mesh=mesh, in_specs=in_specs, out_specs=P("ctx", "ch"), check_vma=False
    )
```

```python
import functools

import jax
import jax.numpy as jnp
from jax import lax
from jax.experimental import pallas as pl
from jax.experimental.pallas import tpu as pltpu
from jax.sharding import PartitionSpec as P

F32 = jnp.float32
BF16 = jnp.bfloat16
MESH = pl.DeviceIdType.MESH

TOKENS = 128
WIDTH = 1024
STRETCH = 64
REACH = 6
TAPS = 7
ORDER = 16
OWNERS = 64
GROUP = 16
SLOTS = 128
PAD = 8
EPS = 1e-05
FULL = 32000.0
TINY = 1e-30


def iota(shape, dim):
    return lax.broadcasted_iota(jnp.int32, shape, dim)


def swap_groups(regs):
    regs = list(regs)
    group = iota((8, 128), 1) // GROUP
    for bit in (1, 2, 4):
        low = (group & bit) == 0
        for i in range(8):
            if i & bit:
                continue
            x, y = regs[i], regs[i | bit]
            regs[i] = jnp.where(low, x, pltpu.roll(y, GROUP * bit, 1))
            regs[i | bit] = jnp.where(low, pltpu.roll(x, 128 - GROUP * bit, 1), y)
    return regs


def one_minus_exp_neg(x):
    series = 1.0 - x / 9.0
    for n in (8, 7, 6, 5, 4, 3, 2):
        series = 1.0 - (x / n) * series
    return jnp.where(x < 0.3, x * series, 1.0 - jnp.exp(-x))


def kernel(
    n_ch,
    width_all,
    q_hbm,
    k_hbm,
    v_hbm,
    sos_hbm,
    sw_hbm,
    rates_hbm,
    res_hbm,
    skip_hbm,
    gain_hbm,
    o_ref,
    q_ref,
    k_ref,
    v_ref,
    sos_ref,
    sw_ref,
    rates_ref,
    res_ref,
    skip_ref,
    gain_ref,
    ext,
    u_s,
    y_s,
    z_s,
    zn_s,
    rt,
    am,
    sw,
    filt,
    stage,
    stage_e,
    own,
    six,
    gather,
    scatter,
    powers,
    mm,
    m1,
    extra,
    rows_s,
    codes_s,
    scan_s,
    scale_s,
    sq_s,
    send_b,
    recv_b,
    send_e,
    recv_e,
    send_s,
    recv_s,
    sq_send,
    sq_recv,
    ssem,
    rsem,
    isem,
):
    me = lax.axis_index("ctx")
    my_ch = lax.axis_index("ch")
    my_z, my_l = me // 4, me % 4
    my_sub, my_lg = me // 8, me % 8

    barrier = pltpu.get_barrier_semaphore()

    def peer_z(step):
        return (my_z + (2 * (step % 2) - 1) * ((step + 1) // 2) + 16) % 16

    def greet(d):
        pl.semaphore_signal(barrier, 1, device_id={"ctx": d}, device_id_type=MESH)

    @pl.loop(0, 15)
    def _(i):
        for l in range(4):
            greet(peer_z(15 - i) * 4 + l)

    for l in range(1, 4):
        greet(my_z * 4 + (my_l + l) % 4)

    @pl.loop(1, n_ch)
    def _(i):
        pl.semaphore_signal(
            barrier, 1, device_id={"ch": (my_ch + i) % n_ch}, device_id_type=MESH
        )

    def load(i, src, dst):
        copy = pltpu.make_async_copy(src, dst, isem.at[i])
        copy.start()
        return copy

    loads = {
        "rates": load(0, rates_hbm, rates_ref),
        "res": load(1, res_hbm, res_ref),
        "sw": load(2, sw_hbm, sw_ref),
        "k": load(3, k_hbm, k_ref),
        "v": load(4, v_hbm, v_ref),
        "q": load(5, q_hbm, q_ref),
        "sos": load(6, sos_hbm, sos_ref),
        "skip": load(7, skip_hbm, skip_ref),
        "gain": load(8, gain_hbm, gain_ref),
    }

    def send_one(src, dst, sem, d):
        pltpu.make_async_remote_copy(
            src_ref=src.at[d],
            dst_ref=dst.at[me],
            send_sem=ssem.at[sem],
            recv_sem=rsem.at[sem],
            device_id={"ctx": d},
            device_id_type=MESH,
        ).start()

    def send_all(*sets):
        @pl.loop(0, 15)
        def _(i):
            for l in range(4):
                for one in sets:
                    send_one(*one, peer_z(15 - i) * 4 + ((my_l // 2) * 2 + 2 + l) % 4)

        for l in range(1, 4):
            for one in sets:
                send_one(*one, my_z * 4 + (my_l + l) % 4)

    def all_of(src, dst, sem):
        return pltpu.make_async_remote_copy(
            src_ref=src.at[pl.ds(0, OWNERS - 1)],
            dst_ref=dst.at[pl.ds(0, OWNERS - 1)],
            send_sem=ssem.at[sem],
            recv_sem=rsem.at[sem],
            device_id={"ctx": (me + 1) % OWNERS},
            device_id_type=MESH,
        )

    def code(x):
        return x.astype(jnp.int32).astype(jnp.int16)

    def uncode(x):
        return x.astype(jnp.int32).astype(F32)

    def narrow(x):
        return x.astype(BF16)

    def widen(x):
        return x.astype(F32)

    def stage_to_send(dst, pitch, first, convert, stage=stage):
        rows = dst.shape[1]

        @pl.loop(0, 8)
        def _(b):
            for i in range(8):
                d = b * 8 + i
                dst[d] = convert(stage[pl.ds(d * pitch + first, rows), :])

    def recv_to_stage(src, pitch, first, convert, stage=stage):
        rows = src.shape[1]

        @pl.loop(0, 8)
        def _(b):
            for i in range(8):
                d = b * 8 + i
                stage[pl.ds(d * pitch + first, rows), :] = convert(src[d])

    def token(array, slot, t):
        return ext[array, pl.ds(pl.multiple_of((slot * STRETCH + t) * 8, 8), 8), :]

    def row8(ref, i):
        return ref[pl.ds(pl.multiple_of(i * 8, 8), 8), :]

    loads["rates"].wait()
    loads["res"].wait()
    loads["sw"].wait()
    for j in range(8):
        lanes = slice(128 * j, 128 * j + 128)
        rate = rates_ref[:, lanes]
        amount = res_ref[:, lanes] * jnp.sqrt(one_minus_exp_neg(2.0 * rate))
        rt[pl.ds(j, ORDER, stride=8), :] = rate
        am[pl.ds(j, ORDER, stride=8), :] = amount
        for a in range(3):
            sw[pl.ds(a * 64 + j, TAPS, stride=8), :] = sw_ref[a, :, lanes]
    for a in range(3):
        sw[a * 64 + 56 : a * 64 + 64, :] = jnp.zeros((8, 128), F32)

    for array, name, ref in ((1, "k", k_ref), (2, "v", v_ref), (0, "q", q_ref)):
        loads[name].wait()
        for slot in range(2):

            @pl.loop(0, 4)
            def _(tb):
                for j in range(8):
                    rows = ref[
                        pl.ds(pl.multiple_of(slot * STRETCH + tb * 16, 16), 16),
                        128 * j : 128 * j + 128,
                    ].astype(F32)
                    start = (slot * STRETCH + tb * 16) * 8 + j
                    ext[array, pl.ds(start, 16, stride=8), :] = rows
    loads["sos"].wait()
    loads["skip"].wait()
    loads["gain"].wait()

    def feature(array, slot, t):
        total = row8(sw, array * 8) * token(array, slot, t)
        for j in range(1, TAPS):
            total = total + row8(sw, array * 8 + j) * token(array, slot, t - j)
        return total

    def u_row(slot, t):
        return pl.ds(pl.multiple_of((slot * STRETCH + t) * 8, 8), 8)

    decay = [jnp.exp(-row8(rt, m)) for m in range(ORDER)]
    end_scale = []
    for slot in range(2):

        def step(t, acc):
            u = feature(1, slot, t) * feature(2, slot, t)
            u_s[u_row(slot, t), :] = u
            return tuple(a * d + u for a, d in zip(acc, decay))

        ends = lax.fori_loop(
            REACH,
            STRETCH,
            step,
            tuple(jnp.zeros((8, 128), F32) for _ in range(ORDER)),
            unroll=2,
        )
        largest = jnp.abs(ends[0])
        for end in ends[1:]:
            largest = jnp.maximum(largest, jnp.abs(end))
        scale = jnp.maximum(largest * 1.0078125, TINY).astype(BF16).astype(F32)
        end_scale.append(scale)
        inverse = FULL / scale
        ends = [jnp.round(end * inverse) for end in ends]
        for h in range(2):
            for lg, reg in enumerate(swap_groups(ends[8 * h : 8 * h + 8])):
                stage[pl.ds(lg * 4 + slot * 2 + h, 8, stride=32), :] = reg
    stage_to_send(send_e, 4, 0, code)

    for slot in range(2):
        q_tail = [token(0, slot, 58 + t) for t in range(6)]
        kinds = (
            [token(1, slot, t) for t in range(6)] + q_tail[4:6],
            [token(2, slot, t) for t in range(6)] + [end_scale[slot]] * 2,
            q_tail[0:2] + [token(1, slot, 58 + t) for t in range(6)],
            q_tail[2:4] + [token(2, slot, 58 + t) for t in range(6)],
        )
        for kind in range(4):
            for lg, reg in enumerate(swap_groups(kinds[kind])):
                stage[pl.ds(lg * 8 + slot * 4 + kind, 8, stride=64), :] = reg
    stage_to_send(send_b, 8, 0, narrow)

    pl.semaphore_wait(barrier, OWNERS - 1 + n_ch - 1)
    send_all((send_b, recv_b, 0), (send_e, recv_e, 1))
    recv_b[me] = send_b[me]
    recv_e[me] = send_e[me]

    def ones_where(hit):
        return jnp.where(hit, 1.0, 0.0).astype(BF16)

    sos_row = jnp.broadcast_to(sos_ref[...], (16, SLOTS))
    sublane = iota((16, SLOTS), 0)
    for b in range(16):
        s = sublane + (16 * b - (129 if b >= 8 else 0))
        gather[16 * b : 16 * b + 16, :] = ones_where(sos_row == s)
    sos_column = jnp.transpose(jnp.broadcast_to(sos_ref[...].astype(F32), (SLOTS, SLOTS)))
    scatter[...] = ones_where(sos_column.astype(jnp.int32) == iota((SLOTS, SLOTS), 1))

    filt[0 : PAD * 8, :] = jnp.zeros((PAD * 8, 128), F32)

    def filter_step(d, powers):
        sums = list(powers)
        while len(sums) > 1:
            sums = [x + y for x, y in zip(sums[0::2], sums[1::2])]
        filt[pl.ds(pl.multiple_of((d + PAD) * 8, 8), 8), :] = sums[0]
        return tuple(p * x for p, x in zip(powers, decay))

    lax.fori_loop(
        0, STRETCH, filter_step, tuple(row8(am, m) for m in range(ORDER)), unroll=2
    )
    filt[PAD * 8 : PAD * 8 + 8, :] = filt[PAD * 8 : PAD * 8 + 8, :] + skip_ref[...]

    for slot in range(2):

        for t in range(REACH):
            total = row8(sw, 0) * token(0, slot, t)
            for j in range(1, t + 1):
                total = total + row8(sw, j) * token(0, slot, t - j)
            z_s[u_row(slot, t), :] = total

        @pl.loop(REACH, STRETCH, unroll=2)
        def _(t):
            z_s[u_row(slot, t), :] = feature(0, slot, t)

    def own_modes(table):
        found = []
        for h in range(2):
            for lg, reg in enumerate(swap_groups([row8(table, 8 * h + m) for m in range(8)])):
                own[lg * 8 : lg * 8 + 8, :] = reg
            found.append(own[pl.ds(my_lg * 8 + my_sub, 1), :])
        return found

    own_rates, own_amounts = own_modes(rt), own_modes(am)

    lane128 = iota((8, 128), 1)

    def own_taps(table, first):
        rows = table[pl.ds(first + my_sub, 8, stride=8), :]
        rows = pltpu.roll(rows, (128 - GROUP * my_lg) % 128, 1)
        rows = jnp.where(lane128 < GROUP, rows, 0.0)
        for shift in (16, 32, 64):
            rows = rows + pltpu.roll(rows, shift, 1)
        return rows

    taps_q, taps_k, taps_v = own_taps(sw, 0), own_taps(sw, 64), own_taps(sw, 128)
    own_filter = own_taps(filt, PAD * 8)
    r_row, r_lane = iota((128, 128), 0), iota((128, 128), 1)
    same = (r_row & (GROUP - 1)) == (r_lane & (GROUP - 1))
    g_row, g_lane = r_row >> 4, r_lane >> 4
    inside = same & (g_row < REACH)

    def split(x):
        upper = x.astype(BF16)
        return upper, (x - upper.astype(F32)).astype(BF16)

    def put_mm(part, x):
        lanes = slice(128 * part, 128 * part + 128)
        mm[0:128, lanes], mm[128:256, lanes] = split(x)
        mm[256:384, lanes] = mm[0:128, lanes]

    for h in range(2):
        lift = jnp.exp(-own_rates[h] * (REACH - 1 - g_row).astype(F32))
        put_mm(h, jnp.where(inside, lift, 0.0))
        rate = jnp.transpose(jnp.broadcast_to(own_rates[h], (128, 128)))
        lift = jnp.exp(-rate * (g_lane + 1).astype(F32))
        lift = jnp.where(same & (g_lane < REACH), lift, 0.0)
        upper, lower = split(lift)
        for i, part in enumerate((upper, lower, upper)):
            m1[256 * i + 128 * h : 256 * i + 128 * h + 128, :] = part
    near = jnp.zeros((128, 128), F32)
    inside = inside & (g_lane < REACH)
    for d in range(REACH):
        near = jnp.where(inside & (g_lane - g_row == d), own_filter[d : d + 1], near)
    put_mm(2, near)
    sub8 = iota((8, 128), 0)
    for h in range(2):
        span = own_rates[h] * float(STRETCH)
        for i, d in enumerate((1, 2, 4)):
            powers[h, 8 * i : 8 * i + 8, :] = jnp.where(sub8 >= d, jnp.exp(-span * float(d)), 0.0)
        powers[h, 24:32, :] = jnp.exp(-span * (sub8 + 1).astype(F32))
        powers[h, 32:40, :] = jnp.broadcast_to(jnp.exp(-span * 8.0), (8, 128))
        powers[h, 40:41, :] = jnp.exp(-own_rates[h] * float(STRETCH - REACH))
        powers[h, 41:42, :] = jnp.exp(-own_rates[h] * float(REACH))
        powers[h, 42:43, :] = own_amounts[h]

    def halves(x):
        hi = jnp.floor(x * (1.0 / 256.0))
        return hi, x - 256.0 * hi

    def group_max(x):
        for shift in (16, 32, 64):
            x = jnp.maximum(x, pltpu.roll(x, shift, 1))
        return x

    def power_of(largest):
        return jnp.ceil(jnp.log2(jnp.maximum(largest, TINY)))

    def encode(x, power):
        return jnp.round(x * (jnp.exp2(-power) * FULL))

    def put(kind, rows, x):
        hi, lo = halves(x)
        at = pl.ds(rows, x.shape[0])
        codes_s[at, kind * 256 : kind * 256 + 128] = hi.astype(BF16)
        codes_s[at, kind * 256 + 128 : kind * 256 + 256] = lo.astype(BF16)

    all_of(send_b, recv_b, 0).wait_recv()
    recv_to_stage(recv_b, 8, 0, widen)
    all_of(send_e, recv_e, 1).wait_recv()
    recv_to_stage(recv_e, 4, 0, uncode, stage_e)
    raw = jnp.concatenate(
        [stage[pl.ds(kind, SLOTS, stride=4), :].astype(BF16) for kind in range(4)], axis=1
    )
    rows_s[0:128, 0:256] = jnp.dot(gather[0:128, :], raw[:, 0:256], preferred_element_type=F32)
    rows_s[128:256, :] = jnp.dot(gather[128:256, :], raw, preferred_element_type=F32)
    group = iota((16, 128), 1) >> 4

    for b in range(8):
        first = b * 16

        def block(kind, before):
            at = pl.ds(before * 128 + b * 16, 16)
            return rows_s[at, kind * 128 : kind * 128 + 128]

        def edge(head, tail, taps):
            total = taps[0:1] * head
            for j in range(1, TAPS):
                mixed = jnp.where(group < 8 - j, head, tail)
                total = total + taps[j : j + 1] * pltpu.roll(mixed, GROUP * j, 1)
            return total

        rows = pl.ds(first, 16)
        head_v, tail_k, tail_v = block(1, 0), block(2, 1), block(3, 1)
        six[rows, :] = edge(block(0, 0), tail_k, taps_k) * edge(head_v, tail_v, taps_v)
        scale = jnp.where(group == 6, head_v * (1.0 / FULL), 0.0)
        for shift in (16, 32, 64):
            scale = scale + pltpu.roll(scale, shift, 1)
        scale_s[rows, :] = scale
        tail_q = jnp.where(group >= 4, pltpu.roll(tail_v, 64, 1), pltpu.roll(tail_k, 32, 1))
        tail_q = jnp.where(group >= 6, block(0, 1), tail_q)
        part = edge(jnp.zeros_like(tail_q), tail_q, taps_q)
        part = jnp.where(group < REACH, part, 0.0)
        power = power_of(group_max(jnp.abs(part)))
        put(3, first, jnp.where(group == 6, power, encode(part, power)))

    upper, lower = split(six[...])
    wide = jnp.concatenate([upper, upper, lower], axis=1)
    extra[...] = jnp.dot(wide, mm[...], preferred_element_type=F32)

    parts = []
    for h in range(2):
        parts += [x.astype(BF16) for x in halves(stage_e[pl.ds(h, SLOTS, stride=2), :])]
    both = jnp.concatenate(parts, axis=1)
    both = jnp.dot(gather[0:128, :], both, preferred_element_type=F32)
    for h in range(2):
        lanes = slice(128 * h, 128 * h + 128)
        codes = both[:, 256 * h : 256 * h + 128] * 256.0 + both[:, 256 * h + 128 : 256 * h + 256]
        x = codes * scale_s[...] + extra[:, lanes] * powers[h, 40:41, :]
        blocks = [x[8 * b : 8 * b + 8] for b in range(16)]
        for i, d in enumerate((1, 2, 4)):
            mult = powers[h, 8 * i : 8 * i + 8, :]
            blocks = [x + mult * pltpu.roll(x, d, 0) for x in blocks]
        lift, whole = powers[h, 24:32, :], powers[h, 32:40, :]
        carry = jnp.zeros((8, 128), F32)
        scan_s[h, 0:8, :] = carry
        for b in range(16):
            total = jnp.broadcast_to(blocks[b][7:8], (8, 128))
            scan_s[h, 8 * b + 1 : 8 * b + 9, :] = blocks[b] + lift * carry
            carry = whole * carry + total
    start = [scan_s[h, 0:128, :] * powers[h, 42:43, :] for h in range(2)]
    upper, lower = split(jnp.concatenate(start, axis=1))
    wide = jnp.concatenate([upper, upper, lower], axis=1)
    rows_s[0:128, 0:128] = extra[:, 256:384] + jnp.dot(
        wide, m1[...], preferred_element_type=F32
    )
    late = [
        start[h] * powers[h, 41:42, :]
        + extra[:, 128 * h : 128 * h + 128] * powers[h, 42:43, :]
        for h in range(2)
    ]
    for b in range(8):
        rows = slice(16 * b, 16 * b + 16)
        power = power_of(
            group_max(jnp.maximum(jnp.abs(late[0][rows]), jnp.abs(late[1][rows])))
        )
        for h in range(2):
            put(h, 16 * b, encode(late[h][rows], power))
        y = rows_s[rows, 0:128]
        power_y = power_of(group_max(jnp.abs(y)))
        y = jnp.where(group == 6, power, jnp.where(group == 7, power_y, encode(y, power_y)))
        put(2, 16 * b, y)
    both = jnp.dot(scatter[...], codes_s[...], preferred_element_type=F32)
    for kind in range(4):
        hi = both[:, 256 * kind : 256 * kind + 128]
        lo = both[:, 256 * kind + 128 : 256 * kind + 256]
        stage[pl.ds(kind, SLOTS, stride=4), :] = hi * 256.0 + lo
    stage_to_send(send_s, 8, 0, code)
    send_all((send_s, recv_s, 2))
    recv_s[me] = send_s[me]

    for b in range(8):
        t0 = b * 8

        def inner(s, acc):
            taps = [row8(filt, t0 + i - s + PAD) for i in range(8)]
            out = []
            for slot in range(2):
                u = u_s[u_row(slot, s), :]
                out += [acc[slot * 8 + i] + taps[i] * u for i in range(8)]
            return tuple(out)

        acc = lax.fori_loop(
            REACH,
            t0 + 8,
            inner,
            tuple(jnp.zeros((8, 128), F32) for _ in range(16)),
            unroll=2,
        )
        for slot in range(2):
            for i in range(8):
                y_s[u_row(slot, t0 + i), :] = acc[slot * 8 + i]

    all_of(send_s, recv_s, 2).wait_recv()
    recv_to_stage(recv_s, 8, 0, uncode)
    for slot in range(2):
        low, high, y_part, q_part = [
            swap_groups(
                [stage[pl.ds(lg * 8 + slot * 4 + kind, 8, stride=64), :] for lg in range(8)]
            )
            for kind in range(4)
        ]
        scale = jnp.exp2(y_part[6]) * (1.0 / FULL)
        scale_y = jnp.exp2(y_part[7]) * (1.0 / FULL)
        scale_q = jnp.exp2(q_part[6]) * (1.0 / FULL)
        for t in range(REACH):
            rows = u_row(slot, t)
            query = z_s[rows, :] + q_part[t] * scale_q
            z_s[rows, :] = query * (y_part[t] * scale_y)

        def last(t, state):
            state = tuple(x * d for x, d in zip(state, decay))
            sums = list(state)
            while len(sums) > 1:
                sums = [x + y for x, y in zip(sums[0::2], sums[1::2])]
            rows = u_row(slot, t)
            z_s[rows, :] = z_s[rows, :] * (y_s[rows, :] + sums[0])
            return state

        state = lax.fori_loop(
            REACH, STRETCH - 2, last, tuple(x * scale for x in low + high), unroll=4
        )
        for t in (STRETCH - 2, STRETCH - 1):
            state = last(t, state)

    @pl.loop(0, 16, unroll=4)
    def _(b):
        rows = pl.ds(pl.multiple_of(b * 8, 8), 8)
        squares = []
        for j in range(8):
            z = z_s[pl.ds(b * 64 + j, 8, stride=8), :]
            lanes = slice(128 * j, 128 * j + 128)
            zn_s[rows, lanes] = z * gain_ref[:, lanes]
            squares.append(z * z)
        while len(squares) > 1:
            squares = [x + y for x, y in zip(squares[0::2], squares[1::2])]
        sq_s[rows, :] = squares[0]

    sums = lax.dot_general(
        jnp.ones((8, 256), BF16),
        jnp.concatenate(split(sq_s[...]), axis=1),
        (((1,), (1,)), ((), ())),
        preferred_element_type=F32,
    )
    sq_send[0] = sums[0:1]
    sq_recv[my_ch] = sums[0:1]

    @pl.loop(1, n_ch)
    def _(i):
        pltpu.make_async_remote_copy(
            src_ref=sq_send.at[0],
            dst_ref=sq_recv.at[my_ch],
            send_sem=ssem.at[3],
            recv_sem=rsem.at[3],
            device_id={"ch": (my_ch + i) % n_ch},
            device_id_type=MESH,
        ).start()

    every = pltpu.make_async_remote_copy(
        src_ref=sq_recv.at[pl.ds(0, n_ch - 1)],
        dst_ref=sq_recv.at[pl.ds(0, n_ch - 1)],
        send_sem=ssem.at[3],
        recv_sem=rsem.at[3],
        device_id={"ch": (my_ch + 1) % n_ch},
        device_id_type=MESH,
    )
    every.wait_recv()
    total = sq_recv[0]
    for i in range(1, n_ch):
        total = total + sq_recv[i]
    scale = lax.rsqrt(total / float(width_all) + EPS)
    sq_s[...] = jnp.transpose(jnp.broadcast_to(scale, (128, 128)))

    @pl.loop(0, 8, unroll=2)
    def _(b):
        rows = pl.ds(pl.multiple_of(b * 16, 16), 16)
        by = sq_s[rows, :]
        for j in range(8):
            lanes = slice(128 * j, 128 * j + 128)
            o_ref[rows, lanes] = (zn_s[rows, lanes] * by).astype(BF16)

    all_of(send_b, recv_b, 0).wait_send()
    all_of(send_e, recv_e, 1).wait_send()
    all_of(send_s, recv_s, 2).wait_send()
    every.wait_send()


def on_device(n_ch, width_all, q_in, k_in, v_in, stretch_of_slot, short_weight, rates, residues, skip, gain):
    vmem = pl.BlockSpec(memory_space=pltpu.VMEM)
    hbm = pl.BlockSpec(memory_space=pltpu.HBM)
    f32 = lambda *shape: pltpu.VMEM(shape, F32)
    bf16 = lambda *shape: pltpu.VMEM(shape, BF16)
    i16 = lambda *shape: pltpu.VMEM(shape, jnp.int16)
    scratch = (
        [bf16(TOKENS, WIDTH)] * 3
        + [pltpu.VMEM((1, SLOTS), jnp.int32), f32(3, TAPS, WIDTH)]
        + [f32(ORDER, WIDTH)] * 2
        + [f32(8, 128), f32(1, WIDTH)]
        + [f32(3, TOKENS * 8, 128)]
        + [f32(TOKENS * 8, 128)] * 3
        + [f32(TOKENS, WIDTH)]
        + [f32(ORDER * 8, 128)] * 2
        + [f32(192, 128), f32((STRETCH + PAD) * 8, 128), f32(512, 128), f32(256, 128), f32(64, 128), f32(128, 128)]
        + [bf16(256, 128), bf16(128, 128), f32(2, 48, 128)]
        + [bf16(384, 384), bf16(768, 128), f32(128, 384), f32(256, 512), bf16(128, 1024)]
        + [f32(2, 136, 128), f32(128, 128), f32(128, 128)]
        + [bf16(OWNERS, 8, 128)] * 2
        + [i16(OWNERS, 4, 128)] * 2
        + [i16(OWNERS, 8, 128)] * 2
        + [f32(1, 1, 128), f32(n_ch, 1, 128)]
        + [pltpu.SemaphoreType.DMA((4,)), pltpu.SemaphoreType.DMA((4,))]
        + [pltpu.SemaphoreType.DMA((9,))]
    )
    return pl.pallas_call(
        functools.partial(kernel, n_ch, width_all),
        out_shape=pltpu.VMEM((TOKENS, WIDTH), BF16),
        in_specs=[hbm] * 9,
        out_specs=vmem,
        scratch_shapes=scratch,
        compiler_params=pltpu.CompilerParams(collective_id=0, has_side_effects=True),
        name="hyena",
    )(
        q_in,
        k_in,
        v_in,
        stretch_of_slot.reshape(1, SLOTS),
        short_weight,
        rates,
        residues,
        skip.reshape(8, 128),
        gain.reshape(1, WIDTH),
    )


def solution(mesh):
    n_ch = mesh.shape["ch"]

    def body(*args):
        return on_device(n_ch, n_ch * WIDTH, *args)

    in_specs = (
        P("ctx", "ch"),
        P("ctx", "ch"),
        P("ctx", "ch"),
        P(),
        P(None, None, "ch"),
        P(None, "ch"),
        P(None, "ch"),
        P("ch"),
        P("ch"),
    )
    return jax.shard_map(
        body, mesh=mesh, in_specs=in_specs, out_specs=P("ctx", "ch"), check_vma=False
    )
```
